512 devices in a mesh: replica: 8 (over y, x_lo), mp: 64 (over z, x_hi, core).
Axes of the slice: x: 4 (x_hi: 2, x_lo: 2; x = x_hi * 2 + x_lo), y: 4, z: 16, core: 2. Of those that a mesh axis runs over, the one named last changes fastest.
Arguments:
- owner_shard: int32 [1024, 256], P(('replica', 'mp')), may hold values from 0 to 63, as said below
- slot_index: int32 [1024, 256], P(('replica', 'mp')), may hold values from 0 to 127
- lengths: int32 [1024], P(('replica', 'mp')), may hold values from 32 to 256
- labels: float32 [1024, 256], P(('replica', 'mp')), may hold values from 0 to 1
- embed_table: bfloat16 [131072, 256], P('mp'), may hold values from -3 to 3
- accumulator: float32 [131072], P('mp'), may hold values from 0.1 to 10
- touched: int32 [8192], P('mp'), may hold values from 0 to 2047, as said below
- w_in: bfloat16 [256, 1024], replicated, may hold values from -0.375 to 0.375
- w_mid: bfloat16 [1024, 1024], replicated, may hold values from -0.1875 to 0.1875
- norm_gain: float32 [1024], replicated, may hold values from 0.5 to 2
- w_out: float32 [1024], replicated, may hold values from -0.1875 to 0.1875
Outputs:
- table_out: bfloat16 [131072, 256], P('mp')
- accum_out: float32 [131072], P('mp')
The draws below stay inside these ranges and needn't reach their ends.
Inputs may be any that keep to these rules, and one draw needn't show every extreme that they name: `owner_shard`: among the events of one device, every shard is named at most 16 times, and one shard, the same for all devices, is named exactly 16 times by every device. `touched`: the 128 entries of each shard are distinct rows of that shard.
All inputs are finite; a program needn't handle non-finite values.
Results may differ from the reference program's by a relative error of at most 0.0034.
Values may be sent and summed in bfloat16 or wider, within the bound.
A program may use at most 64 MiB of HBM per device.

```python
import math
import jax
import jax.numpy as jnp
import numpy as np
from jax import lax

E = 256
H = 1024
ROWS_SHARD = 2048
TOUCH = 128
LEN = 256
SAMP_DEV = 2
CAP = 16
SAMPLES = 1024
VOCAB = 131072
N_REPLICA = 8
N_MP = 64


def draw_owner_shard(key, part):
    block_count = N_REPLICA * N_MP
    events = SAMP_DEV * LEN
    grid_size = N_MP * CAP
    hot_shard = jax.random.randint(jax.random.fold_in(key, 7), (), 0, N_MP)
    block_keys = jax.random.split(jax.random.fold_in(key, 11), block_count)

    def one_block(block_key):
        key_score, key_order = jax.random.split(block_key)
        grid = jnp.arange(grid_size, dtype=jnp.int32)
        grid_owner = grid // CAP
        scores = jax.random.randint(key_score, (grid_size,), 0, 1 << 18) * grid_size + grid
        scores = jnp.where(grid_owner == hot_shard, -1 - grid, scores)
        order = jnp.argsort(scores)
        chosen = grid_owner[order[:events]]
        return jax.random.permutation(key_order, chosen)
    return jax.vmap(one_block)(block_keys).reshape(SAMPLES, LEN).astype(jnp.int32)


def draw_touched(key, part):
    shard_keys = jax.random.split(jax.random.fold_in(key, 3), N_MP)

    def one_shard(shard_key):
        return jax.random.permutation(shard_key, ROWS_SHARD)[:TOUCH]
    return jax.vmap(one_shard)(shard_keys).reshape(N_MP * TOUCH).astype(jnp.int32)


def with_ends(array, own_key, smallest, high):
    longest = array.shape.index(max(array.shape))
    spots = []
    for shift in (0, 1):
        where = [jax.random.randint(jax.random.fold_in(own_key, axis), (), 0, length) for axis, length in enumerate(array.shape)]
        where[longest] = (where[longest] + shift) % array.shape[longest]
        spots.append(tuple(where))
    return array.at[spots[0]].set(smallest).at[spots[1]].set(high)


def level_of(rng, shape, cuts, smallest, largest):
    factor_of, own = 1.0, jax.random.fold_in(rng, 6)
    for position, shards_of in cuts:
        draws = jnp.exp(jax.random.uniform(jax.random.fold_in(own, position), (shards_of,), jnp.float32, smallest / len(cuts), largest / len(cuts)))
        factor_of = factor_of * jnp.repeat(draws, shape[position] // shards_of).reshape([-1 if axis == position else 1 for axis in range(len(shape))])
    return factor_of


def cumulative_ranks(amount, slope):
    loads = [(1 << 20) // math.isqrt(standing ** slope) + 1 for standing in range(1, amount + 1)]
    spread = 1 + sum(loads) // (1 << 30)
    return np.cumsum(np.array([max(1, weight // spread) for weight in loads]))


def ranked(own_key, extent, number_of, skew):
    table = cumulative_ranks(number_of, skew)
    ticket = jax.random.randint(jax.random.fold_in(own_key, 1), extent, 0, int(table[number_of - 1]))
    standing = jnp.searchsorted(jnp.asarray(table, jnp.int32), ticket, side="right")
    return jax.random.permutation(jax.random.fold_in(own_key, 2), number_of)[standing].astype(jnp.int32)


def bell_draw(rng, dims, width, most, shards=(), held_as=jnp.bfloat16):
    factor_of = level_of(rng, dims, shards, -0.22, 0.18) if shards else 1.0
    drawn = jax.random.normal(rng, dims, jnp.float32) * width * factor_of
    return jnp.minimum(jnp.maximum(drawn, -most), most).astype(held_as)


def setup_inputs(seed: int = 0) -> dict:
    splits = jax.random.split(jax.random.key(seed), 12)
    return {
        "owner_shard": draw_owner_shard(jax.random.fold_in(splits[11], 71), 0),
        "slot_index": with_ends(ranked(splits[1], (SAMPLES, LEN), TOUCH, 2), jax.random.fold_in(splits[1], 3), 0, TOUCH - 1).astype(jnp.int32),
        "lengths": with_ends(jax.random.randint(splits[2], (SAMPLES,), LEN // 8, LEN + 1), jax.random.fold_in(splits[2], 1), LEN // 8, LEN).astype(jnp.int32),
        "labels": jnp.clip(1.0 * jax.random.uniform(splits[3], (SAMPLES, LEN), jnp.float32) ** level_of(splits[3], (SAMPLES, LEN), ((0, 512),), -0.2, 0.2), 0.0, 1.0),
        "embed_table": bell_draw(splits[4], (VOCAB, E), 0.5, 3.0, ((0, 64),)),
        "accumulator": jnp.clip(jnp.exp(math.log(10.0) - 4.6051702 * jax.random.uniform(splits[5], (VOCAB,), jnp.float32) ** level_of(splits[5], (VOCAB,), ((0, 64),), -0.2, 0.2)), 0.1, 10.0),
        "touched": draw_touched(jax.random.fold_in(splits[11], 71), 0),
        "w_in": bell_draw(splits[7], (E, H), E ** -0.5, 0.375),
        "w_mid": bell_draw(splits[8], (H, H), H ** -0.5, 0.1875),
        "norm_gain": jnp.clip(jnp.exp(jax.random.uniform(splits[9], (H,), jnp.float32, math.log(0.5), math.log(2.0))), 0.5, 2.0),
        "w_out": bell_draw(splits[10], (H,), H ** -0.5, 0.1875, (), jnp.float32),
    }


learn_rate = 1.0

def silu_slope(values):
    sigma_val = jax.nn.sigmoid(values)
    return sigma_val * (1.0 + values * (1.0 - sigma_val))

def encoder_grad(looked_up, labels, live_mask, w_in, w_mid, norm_gain, w_out):
    pre_act = jnp.dot(looked_up, w_in, preferred_element_type=jnp.float32)
    hidden = jax.nn.silu(pre_act)
    inv_rms = lax.rsqrt(lax.optimization_barrier(jnp.mean(hidden * hidden, axis=-1, keepdims=True)) + 1e-06)
    normed = (hidden * inv_rms * norm_gain).astype(jnp.bfloat16)
    mixed = jnp.dot(normed, w_mid, preferred_element_type=jnp.float32)
    output = hidden + jax.nn.silu(mixed)
    logits = lax.optimization_barrier(jnp.sum(output * w_out, axis=-1))
    d_logit = (jax.nn.sigmoid(logits) - labels) * live_mask
    d_output = d_logit[:, None] * w_out
    d_mixed = (d_output * silu_slope(mixed)).astype(jnp.bfloat16)
    d_normed = jnp.dot(d_mixed, w_mid.T, preferred_element_type=jnp.float32)
    gained = d_normed * norm_gain
    d_hidden = d_output + inv_rms * gained - hidden * inv_rms ** 3 * lax.optimization_barrier(jnp.mean(hidden * gained, axis=-1, keepdims=True))
    d_pre = (d_hidden * silu_slope(pre_act)).astype(jnp.bfloat16)
    return jnp.dot(d_pre, w_in.T, preferred_element_type=jnp.float32).astype(jnp.bfloat16)

def reference(owner_shard, slot_index, lengths, labels, embed_table, accumulator, touched, w_in, w_mid, norm_gain, w_out):
    owners = owner_shard.reshape(-1).astype(jnp.int32)
    slots = slot_index.reshape(-1).astype(jnp.int32)
    list_pos = owners * TOUCH + slots
    row_id = owners * ROWS_SHARD + touched[list_pos]
    looked_up = embed_table[row_id].reshape(SAMPLES, LEN, E)
    live_mask = (jnp.arange(LEN, dtype=jnp.int32)[None, :] < lengths[:, None]).astype(jnp.float32)

    def one_sample(pieces):
        return encoder_grad(pieces[0], pieces[1], pieces[2], w_in, w_mid, norm_gain, w_out)
    event_grad = lax.map(one_sample, (looked_up, labels, live_mask))
    grad_sum = jax.ops.segment_sum(event_grad.reshape(-1, E).astype(jnp.float32), list_pos, num_segments=N_MP * TOUCH)
    global_rows = (jnp.arange(N_MP, dtype=jnp.int32)[:, None] * ROWS_SHARD + touched.reshape(N_MP, TOUCH)).reshape(-1)
    acc_new = accumulator[global_rows] + lax.optimization_barrier(jnp.sum(grad_sum * grad_sum, axis=1))
    new_rows = embed_table[global_rows].astype(jnp.float32) - learn_rate * grad_sum * lax.rsqrt(acc_new)[:, None]
    table_out = embed_table.at[global_rows].set(new_rows.astype(jnp.bfloat16))
    accum_out = accumulator.at[global_rows].set(acc_new)
    return (table_out, accum_out)
```

```python
import functools

import jax
import jax.numpy as jnp
from jax import lax
from jax.experimental import pallas as pl
from jax.experimental.pallas import tpu as pltpu
from jax.sharding import PartitionSpec as P

MESH = pl.DeviceIdType.MESH
F32 = jnp.float32
BF16 = jnp.bfloat16
learn_rate = 1.0

N_CORE = 2
N_XHI = 2


def split3(values):
    high = values.astype(BF16)
    rest = values - high.astype(F32)
    mid = rest.astype(BF16)
    low = (rest - mid.astype(F32)).astype(BF16)
    return high, mid, low


def dot_nn(a, b):
    return jnp.dot(a, b, preferred_element_type=F32)


def dot_nt(a, b):
    return lax.dot_general(a, b, (((1,), (1,)), ((), ())), preferred_element_type=F32)


def silu_slope(values, sigma_val):
    return sigma_val * (1.0 + values * (1.0 - sigma_val))


def iota(shape, dim):
    return lax.broadcasted_iota(jnp.int32, shape, dim)


def reduce_kernel(
    n_rep,
    n_z,
    owner_hbm,
    slot_hbm,
    len_ref,
    label_hbm,
    table_hbm,
    acc_hbm,
    touched_hbm,
    w_in_hbm,
    w_mid_hbm,
    gain_hbm,
    w_out_hbm,
    rows_ref,
    acc_out_ref,
    owner_v,
    slot_v,
    label_v,
    table_v,
    acc_v,
    touched_v,
    w_in_v,
    w_mid_v,
    gain_v,
    w_out_v,
    in_sem,
    hist,
    core_recv,
    z_send,
    z_recv,
    p_send,
    p_recv,
    core_sem,
    z_sem,
    p_sem,
):
    rep = lax.axis_index("replica")
    mp = lax.axis_index("mp")
    core = lax.rem(mp, N_CORE)
    x_hi = lax.rem(lax.div(mp, N_CORE), N_XHI)
    z = lax.div(mp, N_CORE * N_XHI)

    def mp_of(z_i, x_i, core_i):
        return (z_i * N_XHI + x_i) * N_CORE + core_i

    z_shift = sorted(range(1, n_z), key=lambda s: -min(s, n_z - s))
    z_peers = [lax.rem(z + s, n_z) for s in z_shift]
    p_shift = [(r, x) for r in range(n_rep) for x in range(N_XHI) if (r, x) != (0, 0)]
    p_peers = [(lax.rem(rep + r, n_rep), lax.rem(x_hi + x, N_XHI)) for r, x in p_shift]
    partner = mp_of(z, x_hi, 1 - core)

    barrier = pltpu.get_barrier_semaphore()
    for z_i in z_peers:
        pl.semaphore_signal(
            barrier, inc=1, device_id=(rep, mp_of(z_i, x_hi, core)), device_id_type=MESH
        )
    for rep_i, x_i in p_peers:
        pl.semaphore_signal(
            barrier, inc=1, device_id=(rep_i, mp_of(z, x_i, core)), device_id_type=MESH
        )
    pl.semaphore_signal(barrier, inc=1, device_id=(rep, partner), device_id_type=MESH)

    sources = [
        (owner_hbm, owner_v),
        (slot_hbm, slot_v),
        (label_hbm, label_v),
        (touched_hbm, touched_v),
        (acc_hbm, acc_v),
        (gain_hbm, gain_v),
        (w_out_hbm, w_out_v),
        (table_hbm, table_v),
        (w_in_hbm, w_in_v),
        (w_mid_hbm, w_mid_v),
    ]
    loads = [
        pltpu.make_async_copy(src, dst, in_sem.at[i]) for i, (src, dst) in enumerate(sources)
    ]
    for load in loads:
        load.start()
    for load in loads[:3]:
        load.wait()

    samples, length = owner_v.shape
    events = samples * length
    n_rows = hist.shape[0]
    slots_n = hist.shape[1]
    half = n_rows // 2
    row = iota((n_rows, events), 0)
    kind = lax.rem(row, 2)
    row_x = lax.rem(lax.div(row, 2), N_XHI)
    row_z = lax.rem(lax.div(row, 2 * N_XHI), n_z)
    row_core = lax.div(row, half)
    row_owner = mp_of(row_z, row_x, row_core)

    def flat(ref):
        return jnp.concatenate([ref[s : s + 1, :] for s in range(samples)], axis=1)

    live = jnp.concatenate(
        [(iota((1, length), 1) < len_ref[s]).astype(F32) for s in range(samples)], axis=1
    )
    high, mid, low = (part.astype(F32) for part in split3(flat(label_v)))
    hit = row_owner == flat(owner_v)
    counted = hit & (kind == 0)
    labelled = hit & (kind == 1)
    zero = jnp.zeros((n_rows, events), F32)
    lhs = jnp.concatenate(
        [
            jnp.where(counted, live, jnp.where(labelled, live * high, zero)).astype(BF16),
            jnp.where(labelled, live * mid, zero).astype(BF16),
            jnp.where(labelled, live * low, zero).astype(BF16),
        ],
        axis=1,
    )
    slot_hot = (iota((slots_n, events), 0) == flat(slot_v)).astype(F32).astype(BF16)
    hist[...] = dot_nt(lhs, jnp.concatenate([slot_hot] * 3, axis=1))

    pl.semaphore_wait(barrier, len(z_peers) + len(p_peers) + 1)

    core_copy = pltpu.make_async_remote_copy(
        src_ref=hist.at[pl.ds(pl.multiple_of((1 - core) * half, half), half)],
        dst_ref=core_recv,
        send_sem=core_sem.at[0],
        recv_sem=core_sem.at[1],
        device_id=(rep, partner),
        device_id_type=MESH,
    )
    core_copy.start()

    for load in loads[3:]:
        load.wait()
    rows_n = table_v.shape[0]
    lanes = acc_v.shape[1]
    touched_row = touched_v[...]
    eye = iota((slots_n, slots_n), 0) == iota((slots_n, slots_n), 1)

    def to_column(line):
        return jnp.sum(jnp.where(eye, line, 0.0), axis=1, keepdims=True)

    core_copy.wait_recv()
    own = hist[pl.ds(pl.multiple_of(core * half, half), half), :] + core_recv[...]
    part = half // n_z
    for z_i in range(n_z):
        z_send[z_i] = own[z_i * part : (z_i + 1) * part, :]
    for i, z_i in enumerate(z_peers):
        pltpu.make_async_remote_copy(
            src_ref=z_send.at[z_i],
            dst_ref=z_recv.at[z],
            send_sem=z_sem.at[0],
            recv_sem=z_sem.at[1],
            device_id=(rep, mp_of(z_i, x_hi, core)),
            device_id_type=MESH,
        ).start()
    z_recv[z] = z_send[z]

    touched_col = to_column(touched_row.astype(F32)).astype(jnp.int32)
    pick = (iota((slots_n, rows_n), 1) == touched_col).astype(F32).astype(BF16)
    old_rows = dot_nn(pick, table_v[...])
    gain = gain_v[...]
    w_out = w_out_v[...]
    width = w_out.shape[1]
    pre_act = dot_nn(old_rows.astype(BF16), w_in_v[...])
    sig_pre = jax.nn.sigmoid(pre_act)
    hidden = pre_act * sig_pre
    inv_rms = lax.rsqrt(jnp.sum(hidden * hidden, axis=1, keepdims=True) * (1.0 / width) + 1e-06)
    mixed = dot_nn((hidden * inv_rms * gain).astype(BF16), w_mid_v[...])
    sig_mix = jax.nn.sigmoid(mixed)
    logits = jnp.sum((hidden + mixed * sig_mix) * w_out, axis=1, keepdims=True)
    click = jax.nn.sigmoid(logits)
    d_mixed = (w_out * silu_slope(mixed, sig_mix)).astype(BF16)
    gained = dot_nt(d_mixed, w_mid_v[...]) * gain
    dotted = jnp.sum(hidden * gained, axis=1, keepdims=True) * (1.0 / width)
    d_hidden = w_out + inv_rms * gained - hidden * (inv_rms * inv_rms * inv_rms * dotted)
    d_pre = (d_hidden * silu_slope(pre_act, sig_pre)).astype(BF16)
    unit_grad = dot_nt(d_pre, w_in_v[...])

    lo_col = lax.rem(touched_col, lanes)
    hi_col = lax.div(touched_col, lanes)
    acc_rows = acc_v.shape[0]
    hi_hot = (iota((slots_n, acc_rows), 1) == hi_col).astype(F32).astype(BF16)
    lo_hit = iota((slots_n, lanes), 1) == lo_col
    acc_parts = [dot_nn(hi_hot, piece) for piece in split3(acc_v[...])]
    acc_lines = acc_parts[0] + acc_parts[1] + acc_parts[2]
    old_acc = jnp.sum(jnp.where(lo_hit, acc_lines, 0.0), axis=1, keepdims=True)
    hi_hot_t = (
        (iota((acc_rows, slots_n), 0) == lax.div(touched_row, lanes)).astype(F32).astype(BF16)
    )
    acc_hit = dot_nn(hi_hot_t, lo_hit.astype(F32).astype(BF16)) > 0.5

    pltpu.make_async_copy(
        z_recv.at[pl.ds(0, n_z - 1)], z_recv.at[pl.ds(0, n_z - 1)], z_sem.at[1]
    ).wait()
    column = z_recv[0]
    for z_i in range(1, n_z):
        column = column + z_recv[z_i]
    for x_i in range(N_XHI):
        p_send[x_i] = column[x_i * 2 : x_i * 2 + 2, :]
    mine = x_hi * n_rep + rep
    for i, (rep_i, x_i) in enumerate(p_peers):
        pltpu.make_async_remote_copy(
            src_ref=p_send.at[x_i],
            dst_ref=p_recv.at[mine],
            send_sem=p_sem.at[0],
            recv_sem=p_sem.at[1],
            device_id=(rep_i, mp_of(z, x_i, core)),
            device_id_type=MESH,
        ).start()
    p_recv[mine] = p_send[x_hi]
    n_p = len(p_peers)
    pltpu.make_async_copy(
        p_recv.at[pl.ds(0, n_p)], p_recv.at[pl.ds(0, n_p)], p_sem.at[1]
    ).wait()
    total = p_recv[0]
    for i in range(1, n_p + 1):
        total = total + p_recv[i]

    d_sum = to_column(total[0:1, :]) * click - to_column(total[1:2, :])
    grad = d_sum * unit_grad
    acc_new = old_acc + jnp.sum(grad * grad, axis=1, keepdims=True)
    rows_ref[...] = (old_rows - learn_rate * grad * lax.rsqrt(acc_new)).astype(BF16)
    spread = jnp.where(lo_hit, acc_new, 0.0)
    placed = [dot_nn(hi_hot_t, piece) for piece in split3(spread)]
    acc_out_ref[...] = jnp.where(acc_hit, placed[0] + placed[1] + placed[2], acc_v[...])

    core_copy.wait_send()
    pltpu.make_async_copy(
        z_send.at[pl.ds(0, n_z - 1)], z_send.at[pl.ds(0, n_z - 1)], z_sem.at[0]
    ).wait()
    pltpu.make_async_copy(
        p_recv.at[pl.ds(0, n_p)], p_recv.at[pl.ds(0, n_p)], p_sem.at[0]
    ).wait()


def scatter_kernel(touched_ref, rows_ref, acc_ref, table_ref, table_out_ref, acc_out_ref):
    rows_n, slots_n = table_ref.shape[0], touched_ref.shape[1]
    place = (iota((rows_n, slots_n), 0) == touched_ref[...]).astype(F32)
    hit = jnp.sum(place, axis=1, keepdims=True) > 0.5
    placed = dot_nn(place.astype(BF16), rows_ref[...])
    table_out_ref[...] = jnp.where(hit, placed, table_ref[...].astype(F32)).astype(BF16)
    acc_out_ref[...] = acc_ref[...]


def on_device(
    n_rep,
    n_z,
    owner_shard,
    slot_index,
    lengths,
    labels,
    embed_table,
    accumulator,
    touched,
    w_in,
    w_mid,
    norm_gain,
    w_out,
):
    rows_n, emb = embed_table.shape
    slots_n = touched.shape[0]
    width = w_out.shape[0]
    lanes = 128
    acc2 = accumulator.reshape(rows_n // lanes, lanes)
    touched2 = touched.reshape(1, slots_n)
    any_spec = pl.BlockSpec(memory_space=pl.ANY)
    vmem = pl.BlockSpec(memory_space=pltpu.VMEM)
    smem = pl.BlockSpec(memory_space=pltpu.SMEM)
    n_rows = n_z * N_XHI * N_CORE * 2
    part = n_rows // 2 // n_z
    new_rows, acc_new = pl.pallas_call(
        functools.partial(reduce_kernel, n_rep, n_z),
        out_shape=(
            jax.ShapeDtypeStruct((slots_n, emb), BF16),
            jax.ShapeDtypeStruct(acc2.shape, F32),
        ),
        in_specs=[any_spec, any_spec, smem] + [any_spec] * 8,
        out_specs=(vmem, vmem),
        scratch_shapes=[
            pltpu.VMEM(owner_shard.shape, jnp.int32),
            pltpu.VMEM(slot_index.shape, jnp.int32),
            pltpu.VMEM(labels.shape, F32),
            pltpu.VMEM(embed_table.shape, BF16),
            pltpu.VMEM(acc2.shape, F32),
            pltpu.VMEM(touched2.shape, jnp.int32),
            pltpu.VMEM(w_in.shape, BF16),
            pltpu.VMEM(w_mid.shape, BF16),
            pltpu.VMEM((1, width), F32),
            pltpu.VMEM((1, width), F32),
            pltpu.SemaphoreType.DMA((10,)),
            pltpu.VMEM((n_rows, slots_n), F32),
            pltpu.VMEM((n_rows // 2, slots_n), F32),
            pltpu.VMEM((n_z, part, slots_n), F32),
            pltpu.VMEM((n_z, part, slots_n), F32),
            pltpu.VMEM((N_XHI, 2, slots_n), F32),
            pltpu.VMEM((N_XHI * n_rep, 2, slots_n), F32),
            pltpu.SemaphoreType.DMA((2,)),
            pltpu.SemaphoreType.DMA((2,)),
            pltpu.SemaphoreType.DMA((2,)),
        ],
        compiler_params=pltpu.CompilerParams(
            collective_id=0, has_side_effects=True, vmem_limit_bytes=32 * 1024 * 1024
        ),
        name="reduce",
    )(
        owner_shard,
        slot_index,
        lengths,
        labels,
        embed_table,
        acc2,
        touched2,
        w_in,
        w_mid,
        norm_gain.reshape(1, width),
        w_out.reshape(1, width),
    )
    table_out, accum_out = pl.pallas_call(
        scatter_kernel,
        out_shape=(
            jax.ShapeDtypeStruct(embed_table.shape, BF16),
            jax.ShapeDtypeStruct(acc2.shape, F32),
        ),
        in_specs=[vmem] * 4,
        out_specs=(vmem, vmem),
        compiler_params=pltpu.CompilerParams(vmem_limit_bytes=24 * 1024 * 1024),
        name="scatter",
    )(touched2, new_rows, acc_new, embed_table)
    return (table_out, accum_out.reshape(rows_n))


def solution(mesh):
    n_rep = mesh.shape["replica"]
    n_z = mesh.shape["mp"] // (N_CORE * N_XHI)
    in_specs = (
        P(("replica", "mp"), None),
        P(("replica", "mp"), None),
        P(("replica", "mp")),
        P(("replica", "mp"), None),
        P("mp", None),
        P("mp"),
        P("mp"),
        P(),
        P(),
        P(),
        P(),
    )
    out_specs = (P("mp", None), P("mp"))
    return jax.shard_map(
        functools.partial(on_device, n_rep, n_z),
        mesh=mesh,
        in_specs=in_specs,
        out_specs=out_specs,
        check_vma=False,
    )
```

```python
import functools

import jax
import jax.numpy as jnp
from jax import lax
from jax.experimental import pallas as pl
from jax.experimental.pallas import tpu as pltpu
from jax.sharding import PartitionSpec as P

MESH = pl.DeviceIdType.MESH
F32 = jnp.float32
BF16 = jnp.bfloat16
learn_rate = 1.0

N_CORE = 2
N_XHI = 2


def split3(values):
    high = values.astype(BF16)
    rest = values - high.astype(F32)
    mid = rest.astype(BF16)
    low = (rest - mid.astype(F32)).astype(BF16)
    return high, mid, low


def dot_nn(a, b):
    return jnp.dot(a, b, preferred_element_type=F32)


def dot_nt(a, b):
    return lax.dot_general(a, b, (((1,), (1,)), ((), ())), preferred_element_type=F32)


def silu_slope(values, sigma_val):
    return sigma_val * (1.0 + values * (1.0 - sigma_val))


def iota(shape, dim):
    return lax.broadcasted_iota(jnp.int32, shape, dim)


def reduce_kernel(
    n_rep,
    n_z,
    owner_hbm,
    slot_hbm,
    len_hbm,
    label_hbm,
    table_hbm,
    acc_hbm,
    touched_hbm,
    w_in_hbm,
    w_mid_hbm,
    gain_hbm,
    w_out_hbm,
    rows_ref,
    acc_out_ref,
    owner_v,
    slot_v,
    len_s,
    label_v,
    table_v,
    acc_v,
    touched_v,
    w_in_v,
    w_mid_v,
    gain_v,
    w_out_v,
    in_sem,
    hist,
    core_recv,
    z_send,
    z_recv,
    p_send,
    p_recv,
    core_sem,
    z_sem,
    p_sem,
):
    rep = lax.axis_index("replica")
    mp = lax.axis_index("mp")
    core = lax.rem(mp, N_CORE)
    x_hi = lax.rem(lax.div(mp, N_CORE), N_XHI)
    z = lax.div(mp, N_CORE * N_XHI)

    def mp_of(z_i, x_i, core_i):
        return (z_i * N_XHI + x_i) * N_CORE + core_i

    z_shift = sorted(range(1, n_z), key=lambda s: -min(s, n_z - s))
    z_peers = [lax.rem(z + s, n_z) for s in z_shift]
    p_shift = [(r, x) for r in range(n_rep) for x in range(N_XHI) if (r, x) != (0, 0)]
    p_peers = [(lax.rem(rep + r, n_rep), lax.rem(x_hi + x, N_XHI)) for r, x in p_shift]
    partner = mp_of(z, x_hi, 1 - core)

    barrier = pltpu.get_barrier_semaphore()
    for z_i in z_peers:
        pl.semaphore_signal(
            barrier, inc=1, device_id=(rep, mp_of(z_i, x_hi, core)), device_id_type=MESH
        )
    for rep_i, x_i in p_peers:
        pl.semaphore_signal(
            barrier, inc=1, device_id=(rep_i, mp_of(z, x_i, core)), device_id_type=MESH
        )
    pl.semaphore_signal(barrier, inc=1, device_id=(rep, partner), device_id_type=MESH)

    sources = [
        (owner_hbm, owner_v),
        (slot_hbm, slot_v),
        (label_hbm, label_v),
        (len_hbm, len_s),
        (touched_hbm, touched_v),
        (acc_hbm, acc_v),
        (gain_hbm, gain_v),
        (w_out_hbm, w_out_v),
        (table_hbm, table_v),
        (w_in_hbm, w_in_v),
        (w_mid_hbm, w_mid_v),
    ]
    loads = [
        pltpu.make_async_copy(src, dst, in_sem.at[i]) for i, (src, dst) in enumerate(sources)
    ]
    for load in loads:
        load.start()
    for load in loads[:4]:
        load.wait()

    samples, length = owner_v.shape
    events = samples * length
    n_rows = hist.shape[0]
    slots_n = hist.shape[1]
    half = n_rows // 2
    row = iota((n_rows, events), 0)
    kind = lax.rem(row, 2)
    row_x = lax.rem(lax.div(row, 2), N_XHI)
    row_z = lax.rem(lax.div(row, 2 * N_XHI), n_z)
    row_core = lax.div(row, half)
    row_owner = mp_of(row_z, row_x, row_core)

    def flat(ref):
        return jnp.concatenate([ref[s : s + 1, :] for s in range(samples)], axis=1)

    live = jnp.concatenate(
        [(iota((1, length), 1) < len_s[s]).astype(F32) for s in range(samples)], axis=1
    )
    high, mid, low = (part.astype(F32) for part in split3(flat(label_v)))
    hit = row_owner == flat(owner_v)
    counted = hit & (kind == 0)
    labelled = hit & (kind == 1)
    zero = jnp.zeros((n_rows, events), F32)
    lhs = jnp.concatenate(
        [
            jnp.where(counted, live, jnp.where(labelled, live * high, zero)).astype(BF16),
            jnp.where(labelled, live * mid, zero).astype(BF16),
            jnp.where(labelled, live * low, zero).astype(BF16),
        ],
        axis=1,
    )
    slot_hot = (iota((slots_n, events), 0) == flat(slot_v)).astype(F32).astype(BF16)
    hist[...] = dot_nt(lhs, jnp.concatenate([slot_hot] * 3, axis=1))

    pl.semaphore_wait(barrier, len(z_peers) + len(p_peers) + 1)

    core_copy = pltpu.make_async_remote_copy(
        src_ref=hist.at[pl.ds(pl.multiple_of((1 - core) * half, half), half)],
        dst_ref=core_recv,
        send_sem=core_sem.at[0],
        recv_sem=core_sem.at[1],
        device_id=(rep, partner),
        device_id_type=MESH,
    )
    core_copy.start()

    for load in loads[4:]:
        load.wait()
    rows_n = table_v.shape[0]
    lanes = acc_v.shape[1]
    touched_row = touched_v[...]
    eye = iota((slots_n, slots_n), 0) == iota((slots_n, slots_n), 1)

    def to_column(line):
        return jnp.sum(jnp.where(eye, line, 0.0), axis=1, keepdims=True)

    core_copy.wait_recv()
    own = hist[pl.ds(pl.multiple_of(core * half, half), half), :] + core_recv[...]
    part = half // n_z
    for z_i in range(n_z):
        z_send[z_i] = own[z_i * part : (z_i + 1) * part, :]
    for i, z_i in enumerate(z_peers):
        pltpu.make_async_remote_copy(
            src_ref=z_send.at[z_i],
            dst_ref=z_recv.at[z],
            send_sem=z_sem.at[0],
            recv_sem=z_sem.at[1],
            device_id=(rep, mp_of(z_i, x_hi, core)),
            device_id_type=MESH,
        ).start()
    z_recv[z] = z_send[z]

    touched_col = to_column(touched_row.astype(F32)).astype(jnp.int32)
    pick = (iota((slots_n, rows_n), 1) == touched_col).astype(F32).astype(BF16)
    old_rows = dot_nn(pick, table_v[...])
    gain = gain_v[...]
    w_out = w_out_v[...]
    width = w_out.shape[1]
    pre_act = dot_nn(old_rows.astype(BF16), w_in_v[...])
    sig_pre = jax.nn.sigmoid(pre_act)
    hidden = pre_act * sig_pre
    inv_rms = lax.rsqrt(jnp.sum(hidden * hidden, axis=1, keepdims=True) * (1.0 / width) + 1e-06)
    mixed = dot_nn((hidden * inv_rms * gain).astype(BF16), w_mid_v[...])
    sig_mix = jax.nn.sigmoid(mixed)
    logits = jnp.sum((hidden + mixed * sig_mix) * w_out, axis=1, keepdims=True)
    click = jax.nn.sigmoid(logits)
    d_mixed = (w_out * silu_slope(mixed, sig_mix)).astype(BF16)
    gained = dot_nt(d_mixed, w_mid_v[...]) * gain
    dotted = jnp.sum(hidden * gained, axis=1, keepdims=True) * (1.0 / width)
    d_hidden = w_out + inv_rms * gained - hidden * (inv_rms * inv_rms * inv_rms * dotted)
    d_pre = (d_hidden * silu_slope(pre_act, sig_pre)).astype(BF16)
    unit_grad = dot_nt(d_pre, w_in_v[...])

    lo_col = lax.rem(touched_col, lanes)
    hi_col = lax.div(touched_col, lanes)
    acc_rows = acc_v.shape[0]
    hi_hot = (iota((slots_n, acc_rows), 1) == hi_col).astype(F32).astype(BF16)
    lo_hit = iota((slots_n, lanes), 1) == lo_col
    acc_parts = [dot_nn(hi_hot, piece) for piece in split3(acc_v[...])]
    acc_lines = acc_parts[0] + acc_parts[1] + acc_parts[2]
    old_acc = jnp.sum(jnp.where(lo_hit, acc_lines, 0.0), axis=1, keepdims=True)
    hi_hot_t = (
        (iota((acc_rows, slots_n), 0) == lax.div(touched_row, lanes)).astype(F32).astype(BF16)
    )
    acc_hit = dot_nn(hi_hot_t, lo_hit.astype(F32).astype(BF16)) > 0.5

    pltpu.make_async_copy(
        z_recv.at[pl.ds(0, n_z - 1)], z_recv.at[pl.ds(0, n_z - 1)], z_sem.at[1]
    ).wait()
    column = z_recv[0]
    for z_i in range(1, n_z):
        column = column + z_recv[z_i]
    for x_i in range(N_XHI):
        p_send[x_i] = column[x_i * 2 : x_i * 2 + 2, :]
    mine = x_hi * n_rep + rep
    for i, (rep_i, x_i) in enumerate(p_peers):
        pltpu.make_async_remote_copy(
            src_ref=p_send.at[x_i],
            dst_ref=p_recv.at[mine],
            send_sem=p_sem.at[0],
            recv_sem=p_sem.at[1],
            device_id=(rep_i, mp_of(z, x_i, core)),
            device_id_type=MESH,
        ).start()
    p_recv[mine] = p_send[x_hi]
    n_p = len(p_peers)
    pltpu.make_async_copy(
        p_recv.at[pl.ds(0, n_p)], p_recv.at[pl.ds(0, n_p)], p_sem.at[1]
    ).wait()
    total = p_recv[0]
    for i in range(1, n_p + 1):
        total = total + p_recv[i]

    d_sum = to_column(total[0:1, :]) * click - to_column(total[1:2, :])
    grad = d_sum * unit_grad
    acc_new = old_acc + jnp.sum(grad * grad, axis=1, keepdims=True)
    rows_ref[...] = (old_rows - learn_rate * grad * lax.rsqrt(acc_new)).astype(BF16)
    spread = jnp.where(lo_hit, acc_new, 0.0)
    placed = [dot_nn(hi_hot_t, piece) for piece in split3(spread)]
    acc_out_ref[...] = jnp.where(acc_hit, placed[0] + placed[1] + placed[2], acc_v[...])

    core_copy.wait_send()
    pltpu.make_async_copy(
        z_send.at[pl.ds(0, n_z - 1)], z_send.at[pl.ds(0, n_z - 1)], z_sem.at[0]
    ).wait()
    pltpu.make_async_copy(
        p_recv.at[pl.ds(0, n_p)], p_recv.at[pl.ds(0, n_p)], p_sem.at[0]
    ).wait()


def scatter_kernel(touched_ref, rows_ref, acc_ref, table_ref, table_out_ref, acc_out_ref):
    rows_n, slots_n = table_ref.shape[0], touched_ref.shape[1]
    place = (iota((rows_n, slots_n), 0) == touched_ref[...]).astype(F32)
    hit = jnp.sum(place, axis=1, keepdims=True) > 0.5
    placed = dot_nn(place.astype(BF16), rows_ref[...])
    table_out_ref[...] = jnp.where(hit, placed, table_ref[...].astype(F32)).astype(BF16)
    acc_out_ref[...] = acc_ref[...]


def on_device(
    n_rep,
    n_z,
    owner_shard,
    slot_index,
    lengths,
    labels,
    embed_table,
    accumulator,
    touched,
    w_in,
    w_mid,
    norm_gain,
    w_out,
):
    rows_n, emb = embed_table.shape
    slots_n = touched.shape[0]
    width = w_out.shape[0]
    lanes = 128
    acc2 = accumulator.reshape(rows_n // lanes, lanes)
    touched2 = touched.reshape(1, slots_n)
    hbm_spec = pl.BlockSpec(memory_space=pltpu.HBM)
    vmem = pl.BlockSpec(memory_space=pltpu.VMEM)
    n_rows = n_z * N_XHI * N_CORE * 2
    part = n_rows // 2 // n_z
    operands = [
        pltpu.with_memory_space_constraint(array, pltpu.HBM)
        for array in (
            owner_shard,
            slot_index,
            lengths,
            labels,
            embed_table,
            acc2,
            touched2,
            w_in,
            w_mid,
            norm_gain.reshape(1, width),
            w_out.reshape(1, width),
        )
    ]
    new_rows, acc_new = pl.pallas_call(
        functools.partial(reduce_kernel, n_rep, n_z),
        out_shape=(
            jax.ShapeDtypeStruct((slots_n, emb), BF16),
            jax.ShapeDtypeStruct(acc2.shape, F32),
        ),
        in_specs=[hbm_spec] * len(operands),
        out_specs=(vmem, vmem),
        scratch_shapes=[
            pltpu.VMEM(owner_shard.shape, jnp.int32),
            pltpu.VMEM(slot_index.shape, jnp.int32),
            pltpu.SMEM(lengths.shape, jnp.int32),
            pltpu.VMEM(labels.shape, F32),
            pltpu.VMEM(embed_table.shape, BF16),
            pltpu.VMEM(acc2.shape, F32),
            pltpu.VMEM(touched2.shape, jnp.int32),
            pltpu.VMEM(w_in.shape, BF16),
            pltpu.VMEM(w_mid.shape, BF16),
            pltpu.VMEM((1, width), F32),
            pltpu.VMEM((1, width), F32),
            pltpu.SemaphoreType.DMA((11,)),
            pltpu.VMEM((n_rows, slots_n), F32),
            pltpu.VMEM((n_rows // 2, slots_n), F32),
            pltpu.VMEM((n_z, part, slots_n), F32),
            pltpu.VMEM((n_z, part, slots_n), F32),
            pltpu.VMEM((N_XHI, 2, slots_n), F32),
            pltpu.VMEM((N_XHI * n_rep, 2, slots_n), F32),
            pltpu.SemaphoreType.DMA((2,)),
            pltpu.SemaphoreType.DMA((2,)),
            pltpu.SemaphoreType.DMA((2,)),
        ],
        compiler_params=pltpu.CompilerParams(
            collective_id=0, has_side_effects=True, vmem_limit_bytes=32 * 1024 * 1024
        ),
        name="reduce",
    )(*operands)
    table_out, accum_out = pl.pallas_call(
        scatter_kernel,
        out_shape=(
            jax.ShapeDtypeStruct(embed_table.shape, BF16),
            jax.ShapeDtypeStruct(acc2.shape, F32),
        ),
        in_specs=[vmem] * 4,
        out_specs=(vmem, vmem),
        compiler_params=pltpu.CompilerParams(vmem_limit_bytes=24 * 1024 * 1024),
        name="scatter",
    )(touched2, new_rows, acc_new, embed_table)
    return (table_out, accum_out.reshape(rows_n))


def solution(mesh):
    n_rep = mesh.shape["replica"]
    n_z = mesh.shape["mp"] // (N_CORE * N_XHI)
    in_specs = (
        P(("replica", "mp"), None),
        P(("replica", "mp"), None),
        P(("replica", "mp")),
        P(("replica", "mp"), None),
        P("mp", None),
        P("mp"),
        P("mp"),
        P(),
        P(),
        P(),
        P(),
    )
    out_specs = (P("mp", None), P("mp"))
    return jax.shard_map(
        functools.partial(on_device, n_rep, n_z),
        mesh=mesh,
        in_specs=in_specs,
        out_specs=out_specs,
        check_vma=False,
    )
```

```python
import functools

import jax
import jax.numpy as jnp
from jax import lax
from jax.experimental import pallas as pl
from jax.experimental.pallas import tpu as pltpu
from jax.sharding import PartitionSpec as P

MESH = pl.DeviceIdType.MESH
F32 = jnp.float32
BF16 = jnp.bfloat16
learn_rate = 1.0

N_CORE = 2
N_XHI = 2
N_XLO = 2
REACH = 4
UP = REACH
DOWN = REACH - 1


def split3(values):
    high = values.astype(BF16)
    rest = values - high.astype(F32)
    mid = rest.astype(BF16)
    low = (rest - mid.astype(F32)).astype(BF16)
    return high, mid, low


def dot_nn(a, b):
    return jnp.dot(a, b, preferred_element_type=F32)


def dot_nt(a, b):
    return lax.dot_general(a, b, (((1,), (1,)), ((), ())), preferred_element_type=F32)


def silu_slope(values, sigma_val):
    return sigma_val * (1.0 + values * (1.0 - sigma_val))


def iota(shape, dim):
    return lax.broadcasted_iota(jnp.int32, shape, dim)


def ring(size, shift):
    return min(shift % size, -shift % size)


def reduce_kernel(
    n_y,
    n_z,
    owner_hbm,
    slot_hbm,
    len_hbm,
    label_hbm,
    table_hbm,
    acc_hbm,
    touched_hbm,
    w_in_hbm,
    w_mid_hbm,
    gain_hbm,
    w_out_hbm,
    rows_ref,
    acc_out_ref,
    place_ref,
    rest_ref,
    owner_v,
    slot_v,
    len_s,
    label_v,
    table_v,
    acc_v,
    touched_v,
    w_in_v,
    w_mid_v,
    gain_v,
    w_out_v,
    in_sem,
    hist,
    far_recv,
    near_send,
    near_recv,
    plane_send,
    plane_recv,
    far_sems,
    far_sent,
    near_sem,
    plane_sem,
):
    rep = lax.axis_index("replica")
    mp = lax.axis_index("mp")
    core = lax.rem(mp, N_CORE)
    x_hi = lax.rem(lax.div(mp, N_CORE), N_XHI)
    z = lax.div(mp, N_CORE * N_XHI)
    y = lax.div(rep, N_XLO)
    n_x = N_XHI * N_XLO
    x = x_hi * N_XLO + lax.rem(rep, N_XLO)

    def column_peer(shift):
        z_i = lax.rem(z + (shift + n_z), n_z)
        return (rep, (z_i * N_XHI + x_hi) * N_CORE + core)

    def block(shift):
        return lax.rem(z + (shift + 2 * n_z), n_z)

    plane = [
        (dy, dx, dc)
        for dy in range(n_y)
        for dx in range(n_x)
        for dc in range(N_CORE)
        if (dy, dx, dc) != (0, 0, 0)
    ]
    plane.sort(key=lambda d: -(ring(n_y, d[0]) + ring(n_x, d[1])))
    plane_peers = []
    for dy, dx, dc in plane:
        y_i, x_i = lax.rem(y + dy, n_y), lax.rem(x + dx, n_x)
        core_i = lax.rem(core + dc, N_CORE)
        xhi_i = lax.div(x_i, N_XLO)
        rep_i = y_i * N_XLO + lax.rem(x_i, N_XLO)
        kind_i = xhi_i * N_CORE + core_i
        plane_peers.append((kind_i, (rep_i, z * (N_XHI * N_CORE) + kind_i)))
    shifts = [s for k in range(REACH, 0, -1) for s in (k, -k)]

    sources = [
        (owner_hbm, owner_v),
        (slot_hbm, slot_v),
        (label_hbm, label_v),
        (len_hbm, len_s),
        (touched_hbm, touched_v),
        (table_hbm, table_v),
        (w_in_hbm, w_in_v),
        (w_mid_hbm, w_mid_v),
        (gain_hbm, gain_v),
        (w_out_hbm, w_out_v),
        (acc_hbm, acc_v),
    ]
    loads = [
        pltpu.make_async_copy(src, dst, in_sem.at[i]) for i, (src, dst) in enumerate(sources)
    ]
    for load in loads[:4]:
        load.start()
    barrier = pltpu.get_barrier_semaphore()
    for shift in shifts:
        pl.semaphore_signal(
            barrier, inc=1, device_id=column_peer(shift), device_id_type=MESH
        )
    for _, peer in plane_peers:
        pl.semaphore_signal(barrier, inc=1, device_id=peer, device_id_type=MESH)
    for load in loads[4:]:
        load.start()

    samples, length = owner_v.shape
    n_rows = n_z * 8
    slots_n = hist.shape[2]
    row = iota((n_rows, slots_n), 0)
    counts = lax.rem(row, 2) == 0
    row_owner = lax.div(row, 2)
    slot_iota = iota((slots_n, slots_n), 0)
    lane = iota((1, slots_n), 1)
    for load in loads[:4]:
        load.wait()
    parts, hots = [[], [], []], []
    for sample in range(samples):
        for start in range(0, length, slots_n):
            window = (slice(sample, sample + 1), slice(start, start + slots_n))
            live = (lane + start < len_s[sample]).astype(F32)
            high, mid, low = (live * part.astype(F32) for part in split3(label_v[window]))
            hit = row_owner == owner_v[window]
            labelled = hit & ~counts
            parts[0].append(jnp.where(hit, jnp.where(counts, live, high), 0.0).astype(BF16))
            parts[1].append(jnp.where(labelled, mid, 0.0).astype(BF16))
            parts[2].append(jnp.where(labelled, low, 0.0).astype(BF16))
            hots.append((slot_iota == slot_v[window]).astype(F32).astype(BF16))
    stacked = jnp.concatenate([jnp.concatenate(part, axis=1) for part in parts], axis=0)
    counted = dot_nt(stacked, jnp.concatenate(hots, axis=1))
    counted = counted[:n_rows] + counted[n_rows : 2 * n_rows] + counted[2 * n_rows :]
    hist[...] = counted.reshape(n_z, 8, slots_n)

    pl.semaphore_wait(barrier, len(shifts) + len(plane_peers))

    def far(k):
        slot = k - 1 if k > 0 else UP - k - 1
        hop = REACH if k > 0 else -REACH
        return pltpu.make_async_remote_copy(
            src_ref=hist.at[block(hop + k)],
            dst_ref=far_recv.at[slot],
            send_sem=far_sent,
            recv_sem=far_sems.at[slot],
            device_id=column_peer(hop),
            device_id_type=MESH,
        )

    order = [s for s in shifts if s != -REACH]
    for k in order:
        far(k).start()

    def near(k, src):
        slot = k - 1 if k > 0 else UP - k - 1
        return pltpu.make_async_remote_copy(
            src_ref=src,
            dst_ref=near_recv.at[slot],
            send_sem=near_sem.at[0],
            recv_sem=near_sem.at[1],
            device_id=column_peer(k),
            device_id_type=MESH,
        )

    near(-REACH, hist.at[block(-REACH)]).start()
    for k in order:
        slot = k - 1 if k > 0 else UP - k - 1
        pltpu.make_async_copy(far_recv.at[slot], far_recv.at[slot], far_sems.at[slot]).wait()
        near_send[slot] = hist[block(k)] + far_recv[slot]
        near(k, near_send.at[slot]).start()

    for load in loads[4:]:
        load.wait()
    rows_n = table_v.shape[0]
    lanes = acc_v.shape[1]
    touched_row = touched_v[...]
    eye = iota((slots_n, slots_n), 0) == iota((slots_n, slots_n), 1)

    def to_column(line):
        return jnp.sum(jnp.where(eye, line, 0.0), axis=1, keepdims=True)

    touched_col = to_column(touched_row.astype(F32)).astype(jnp.int32)
    pick = (iota((slots_n, rows_n), 1) == touched_col).astype(F32).astype(BF16)
    old_rows = dot_nn(pick, table_v[...])
    gain = gain_v[...]
    w_out = w_out_v[...]
    width = w_out.shape[1]
    pre_act = dot_nn(old_rows.astype(BF16), w_in_v[...])
    sig_pre = jax.nn.sigmoid(pre_act)
    hidden = pre_act * sig_pre
    inv_rms = lax.rsqrt(jnp.sum(hidden * hidden, axis=1, keepdims=True) * (1.0 / width) + 1e-06)
    mixed = dot_nn((hidden * inv_rms * gain).astype(BF16), w_mid_v[...])
    sig_mix = jax.nn.sigmoid(mixed)
    logits = jnp.sum((hidden + mixed * sig_mix) * w_out, axis=1, keepdims=True)
    click = jax.nn.sigmoid(logits)
    d_mixed = (w_out * silu_slope(mixed, sig_mix)).astype(BF16)

    pltpu.make_async_copy(near_recv, near_recv, near_sem.at[1]).wait()
    column = hist[z]
    for slot in range(UP + REACH):
        column = column + near_recv[slot]
    n_kind = N_XHI * N_CORE
    for kind in range(n_kind):
        plane_send[kind] = column[kind * 2 : kind * 2 + 2, :]
    own_kind = x_hi * N_CORE + core
    mine = rep * n_kind + own_kind
    for kind_i, peer in plane_peers:
        pltpu.make_async_remote_copy(
            src_ref=plane_send.at[kind_i],
            dst_ref=plane_recv.at[mine],
            send_sem=plane_sem.at[0],
            recv_sem=plane_sem.at[1],
            device_id=peer,
            device_id_type=MESH,
        ).start()
    plane_recv[mine] = plane_send[own_kind]

    gained = dot_nt(d_mixed, w_mid_v[...]) * gain
    dotted = jnp.sum(hidden * gained, axis=1, keepdims=True) * (1.0 / width)
    d_hidden = w_out + inv_rms * gained - hidden * (inv_rms * inv_rms * inv_rms * dotted)
    d_pre = (d_hidden * silu_slope(pre_act, sig_pre)).astype(BF16)
    unit_grad = dot_nt(d_pre, w_in_v[...])

    lo_col = lax.rem(touched_col, lanes)
    hi_col = lax.div(touched_col, lanes)
    acc_rows = acc_v.shape[0]
    hi_hot = (iota((slots_n, acc_rows), 1) == hi_col).astype(F32).astype(BF16)
    lo_hit = iota((slots_n, lanes), 1) == lo_col
    acc_parts = [dot_nn(hi_hot, piece) for piece in split3(acc_v[...])]
    acc_lines = acc_parts[0] + acc_parts[1] + acc_parts[2]
    old_acc = jnp.sum(jnp.where(lo_hit, acc_lines, 0.0), axis=1, keepdims=True)
    hi_hot_t = (
        (iota((acc_rows, slots_n), 0) == lax.div(touched_row, lanes)).astype(F32).astype(BF16)
    )
    acc_hit = dot_nn(hi_hot_t, lo_hit.astype(F32).astype(BF16)) > 0.5

    place = (iota((rows_n, slots_n), 0) == touched_row).astype(F32).astype(BF16)
    place_ref[...] = place
    hits = dot_nn(place, jnp.ones((slots_n, table_v.shape[1]), BF16))
    rest_ref[...] = jnp.where(hits > 0.5, 0.0, table_v[...].astype(F32)).astype(BF16)

    n_p = len(plane_peers)
    pltpu.make_async_copy(
        plane_recv.at[pl.ds(0, n_p)], plane_recv.at[pl.ds(0, n_p)], plane_sem.at[1]
    ).wait()
    total = plane_recv[0]
    for i in range(1, n_p + 1):
        total = total + plane_recv[i]

    d_sum = to_column(total[0:1, :]) * click - to_column(total[1:2, :])
    grad = d_sum * unit_grad
    acc_new = old_acc + jnp.sum(grad * grad, axis=1, keepdims=True)
    rows_ref[...] = (old_rows - learn_rate * grad * lax.rsqrt(acc_new)).astype(BF16)
    spread = jnp.where(lo_hit, acc_new, 0.0)
    placed = [dot_nn(hi_hot_t, piece) for piece in split3(spread)]
    acc_out_ref[...] = jnp.where(acc_hit, placed[0] + placed[1] + placed[2], acc_v[...])

    pltpu.make_async_copy(far_recv, far_recv, far_sent).wait()
    pltpu.make_async_copy(near_recv, near_recv, near_sem.at[0]).wait()
    pltpu.make_async_copy(
        plane_recv.at[pl.ds(0, n_p)], plane_recv.at[pl.ds(0, n_p)], plane_sem.at[0]
    ).wait()


def scatter_kernel(rows_ref, acc_ref, place_ref, rest_ref, table_out, acc_out, tiles, sem):
    acc_copy = pltpu.make_async_copy(acc_ref, acc_out, sem.at[0])
    acc_copy.start()
    rows = rows_ref[...]
    count = tiles.shape[0]
    step = tiles.shape[1]
    copies = []
    for i in range(count):
        span = slice(i * step, (i + 1) * step)
        tiles[i] = (dot_nn(place_ref[span, :], rows) + rest_ref[span, :].astype(F32)).astype(BF16)
        copy = pltpu.make_async_copy(tiles.at[i], table_out.at[pl.ds(i * step, step)], sem.at[i + 1])
        copy.start()
        copies.append(copy)
    for copy in copies:
        copy.wait()
    acc_copy.wait()


def on_device(
    n_y,
    n_z,
    owner_shard,
    slot_index,
    lengths,
    labels,
    embed_table,
    accumulator,
    touched,
    w_in,
    w_mid,
    norm_gain,
    w_out,
):
    rows_n, emb = embed_table.shape
    slots_n = touched.shape[0]
    width = w_out.shape[0]
    lanes = 128
    acc2 = accumulator.reshape(rows_n // lanes, lanes)
    touched2 = touched.reshape(1, slots_n)
    hbm_spec = pl.BlockSpec(memory_space=pltpu.HBM)
    vmem = pl.BlockSpec(memory_space=pltpu.VMEM)
    n_far = UP + DOWN
    n_near = UP + REACH
    n_kind = N_XHI * N_CORE
    operands = [
        pltpu.with_memory_space_constraint(array, pltpu.HBM)
        for array in (
            owner_shard,
            slot_index,
            lengths,
            labels,
            embed_table,
            acc2,
            touched2,
            w_in,
            w_mid,
            norm_gain.reshape(1, width),
            w_out.reshape(1, width),
        )
    ]
    made = pl.pallas_call(
        functools.partial(reduce_kernel, n_y, n_z),
        out_shape=(
            jax.ShapeDtypeStruct((slots_n, emb), BF16),
            jax.ShapeDtypeStruct(acc2.shape, F32),
            jax.ShapeDtypeStruct((rows_n, slots_n), BF16),
            jax.ShapeDtypeStruct((rows_n, emb), BF16),
        ),
        in_specs=[hbm_spec] * len(operands),
        out_specs=(vmem,) * 4,
        scratch_shapes=[
            pltpu.VMEM(owner_shard.shape, jnp.int32),
            pltpu.VMEM(slot_index.shape, jnp.int32),
            pltpu.SMEM(lengths.shape, jnp.int32),
            pltpu.VMEM(labels.shape, F32),
            pltpu.VMEM(embed_table.shape, BF16),
            pltpu.VMEM(acc2.shape, F32),
            pltpu.VMEM(touched2.shape, jnp.int32),
            pltpu.VMEM(w_in.shape, BF16),
            pltpu.VMEM(w_mid.shape, BF16),
            pltpu.VMEM((1, width), F32),
            pltpu.VMEM((1, width), F32),
            pltpu.SemaphoreType.DMA((11,)),
            pltpu.VMEM((n_z, 8, slots_n), F32),
            pltpu.VMEM((n_far, 8, slots_n), F32),
            pltpu.VMEM((n_far, 8, slots_n), F32),
            pltpu.VMEM((n_near, 8, slots_n), F32),
            pltpu.VMEM((n_kind, 2, slots_n), F32),
            pltpu.VMEM((n_kind * n_y * N_XLO, 2, slots_n), F32),
            pltpu.SemaphoreType.DMA((n_far,)),
            pltpu.SemaphoreType.DMA,
            pltpu.SemaphoreType.DMA((2,)),
            pltpu.SemaphoreType.DMA((2,)),
        ],
        compiler_params=pltpu.CompilerParams(
            collective_id=0, has_side_effects=True, vmem_limit_bytes=32 * 1024 * 1024
        ),
        name="reduce",
    )(*operands)
    tiles = 4
    table_out, accum_out = pl.pallas_call(
        scatter_kernel,
        out_shape=(
            jax.ShapeDtypeStruct(embed_table.shape, BF16),
            jax.ShapeDtypeStruct(acc2.shape, F32),
        ),
        in_specs=[vmem] * 4,
        out_specs=(hbm_spec,) * 2,
        scratch_shapes=[
            pltpu.VMEM((tiles, rows_n // tiles, emb), BF16),
            pltpu.SemaphoreType.DMA((tiles + 1,)),
        ],
        compiler_params=pltpu.CompilerParams(vmem_limit_bytes=24 * 1024 * 1024),
        name="scatter",
    )(*made)
    return (table_out, accum_out.reshape(rows_n))


def solution(mesh):
    n_y = mesh.shape["replica"] // N_XLO
    n_z = mesh.shape["mp"] // (N_CORE * N_XHI)
    in_specs = (
        P(("replica", "mp"), None),
        P(("replica", "mp"), None),
        P(("replica", "mp")),
        P(("replica", "mp"), None),
        P("mp", None),
        P("mp"),
        P("mp"),
        P(),
        P(),
        P(),
        P(),
    )
    out_specs = (P("mp", None), P("mp"))
    return jax.shard_map(
        functools.partial(on_device, n_y, n_z),
        mesh=mesh,
        in_specs=in_specs,
        out_specs=out_specs,
        check_vma=False,
    )
```

```python
import functools

import jax
import jax.numpy as jnp
from jax import lax
from jax.experimental import pallas as pl
from jax.experimental.pallas import tpu as pltpu
from jax.sharding import PartitionSpec as P

MESH = pl.DeviceIdType.MESH
F32 = jnp.float32
BF16 = jnp.bfloat16
learn_rate = 1.0

N_CORE = 2
N_XHI = 2
N_XLO = 2
REACH = 4
UP = REACH
DOWN = REACH - 1


def split3(values):
    high = values.astype(BF16)
    rest = values - high.astype(F32)
    mid = rest.astype(BF16)
    low = (rest - mid.astype(F32)).astype(BF16)
    return high, mid, low


def dot_nn(a, b):
    return jnp.dot(a, b, preferred_element_type=F32)


def dot_nt(a, b):
    return lax.dot_general(a, b, (((1,), (1,)), ((), ())), preferred_element_type=F32)


def silu_slope(values, sigma_val):
    return sigma_val * (1.0 + values * (1.0 - sigma_val))


def iota(shape, dim):
    return lax.broadcasted_iota(jnp.int32, shape, dim)


def ring(size, shift):
    return min(shift % size, -shift % size)


def reduce_kernel(
    n_y,
    n_z,
    owner_hbm,
    slot_hbm,
    len_hbm,
    label_hbm,
    table_hbm,
    acc_hbm,
    touched_hbm,
    w_in_hbm,
    w_mid_hbm,
    gain_hbm,
    w_out_hbm,
    rows_ref,
    acc_out_ref,
    place_ref,
    rest_ref,
    owner_v,
    slot_v,
    len_s,
    label_v,
    table_v,
    acc_v,
    touched_v,
    w_in_v,
    w_mid_v,
    gain_v,
    w_out_v,
    in_sem,
    hist,
    far_recv,
    near_send,
    near_recv,
    core_recv,
    plane_send,
    plane_recv,
    far_sems,
    far_sent,
    near_sem,
    core_sem,
    plane_sem,
):
    rep = lax.axis_index("replica")
    mp = lax.axis_index("mp")
    core = lax.rem(mp, N_CORE)
    x_hi = lax.rem(lax.div(mp, N_CORE), N_XHI)
    z = lax.div(mp, N_CORE * N_XHI)
    y = lax.div(rep, N_XLO)
    n_x = N_XHI * N_XLO
    x = x_hi * N_XLO + lax.rem(rep, N_XLO)

    def column_peer(shift, turn=0):
        z_i = lax.rem(z + (shift + n_z), n_z)
        return (rep, (z_i * N_XHI + x_hi) * N_CORE + lax.rem(core + turn, N_CORE))

    def block(shift):
        return lax.rem(z + (shift + 2 * n_z), n_z)

    plane = [(dy, dx) for dy in range(n_y) for dx in range(n_x) if (dy, dx) != (0, 0)]
    plane.sort(key=lambda d: -(ring(n_y, d[0]) + ring(n_x, d[1])))
    plane_peers = []
    for dy, dx in plane:
        y_i, x_i = lax.rem(y + dy, n_y), lax.rem(x + dx, n_x)
        xhi_i = lax.div(x_i, N_XLO)
        rep_i = y_i * N_XLO + lax.rem(x_i, N_XLO)
        plane_peers.append((xhi_i, (rep_i, (z * N_XHI + xhi_i) * N_CORE + core)))
    partner = (rep, mp + 1 - 2 * core)
    shifts = [s for k in range(REACH, 0, -1) for s in (k, -k)]

    sources = [
        (owner_hbm, owner_v),
        (slot_hbm, slot_v),
        (label_hbm, label_v),
        (len_hbm, len_s),
        (touched_hbm, touched_v),
        (table_hbm, table_v),
        (w_in_hbm, w_in_v),
        (w_mid_hbm, w_mid_v),
        (gain_hbm, gain_v),
        (w_out_hbm, w_out_v),
        (acc_hbm, acc_v),
    ]
    loads = [
        pltpu.make_async_copy(src, dst, in_sem.at[i]) for i, (src, dst) in enumerate(sources)
    ]
    barrier = pltpu.get_barrier_semaphore()
    for shift in shifts:
        pl.semaphore_signal(
            barrier, inc=1, device_id=column_peer(shift), device_id_type=MESH
        )
    for load in loads[:4]:
        load.start()
    others = [column_peer(REACH, 1), column_peer(-REACH, 1), partner]
    for peer in others + [peer for _, peer in plane_peers]:
        pl.semaphore_signal(barrier, inc=1, device_id=peer, device_id_type=MESH)
    for load in loads[4:]:
        load.start()

    samples, length = owner_v.shape
    part = hist.shape[1]
    n_rows = hist.shape[0] * part
    slots_n = hist.shape[2]
    row = iota((n_rows, slots_n), 0)
    counts = lax.rem(row, 2) == 0
    row_z = lax.rem(lax.div(row, part), n_z)
    row_x = lax.rem(lax.div(row, 2), N_XHI)
    row_owner = (row_z * N_XHI + row_x) * N_CORE + lax.div(row, n_z * part)
    slot_iota = iota((slots_n, slots_n), 0)
    lane = iota((1, slots_n), 1)
    for load in loads[:4]:
        load.wait()
    parts, hots = [[], [], []], []
    for sample in range(samples):
        for start in range(0, length, slots_n):
            window = (slice(sample, sample + 1), slice(start, start + slots_n))
            live = (lane + start < len_s[sample]).astype(F32)
            high, mid, low = (live * part.astype(F32) for part in split3(label_v[window]))
            hit = row_owner == owner_v[window]
            labelled = hit & ~counts
            parts[0].append(jnp.where(hit, jnp.where(counts, live, high), 0.0).astype(BF16))
            parts[1].append(jnp.where(labelled, mid, 0.0).astype(BF16))
            parts[2].append(jnp.where(labelled, low, 0.0).astype(BF16))
            hots.append((slot_iota == slot_v[window]).astype(F32).astype(BF16))
    stacked = jnp.concatenate([jnp.concatenate(part, axis=1) for part in parts], axis=0)
    counted = dot_nt(stacked, jnp.concatenate(hots, axis=1))
    counted = counted[:n_rows] + counted[n_rows : 2 * n_rows] + counted[2 * n_rows :]
    for i in range(N_CORE * n_z):
        hist[i] = counted[i * part : (i + 1) * part, :]

    pl.semaphore_wait(barrier, len(shifts) + len(plane_peers) + len(others))

    core_copy = pltpu.make_async_remote_copy(
        src_ref=hist.at[pl.ds((1 - core) * n_z, n_z)],
        dst_ref=core_recv,
        send_sem=core_sem.at[0],
        recv_sem=core_sem.at[1],
        device_id=partner,
        device_id_type=MESH,
    )
    core_copy.start()

    def slot_of(k):
        return k - 1 if k > 0 else UP - k - 1

    order = [s for s in shifts if s != -REACH]
    for k in order:
        hop = REACH if k > 0 else -REACH
        for turn in (1, 0):
            pltpu.make_async_remote_copy(
                src_ref=hist.at[lax.rem(core + turn, N_CORE) * n_z + block(hop + k)],
                dst_ref=far_recv.at[slot_of(k), core],
                send_sem=far_sent,
                recv_sem=far_sems.at[slot_of(k)],
                device_id=column_peer(hop, turn),
                device_id_type=MESH,
            ).start()

    core_copy.wait_recv()

    def both(z_i):
        return hist[core * n_z + z_i] + core_recv[z_i]

    for k in [-REACH] + order:
        slot = slot_of(k)
        own = both(block(k))
        if k != -REACH:
            arrived = far_recv.at[slot]
            pltpu.make_async_copy(arrived, arrived, far_sems.at[slot]).wait()
            own = own + (far_recv[slot, 0] + far_recv[slot, 1])
        near_send[slot] = own
        pltpu.make_async_remote_copy(
            src_ref=near_send.at[slot],
            dst_ref=near_recv.at[slot],
            send_sem=near_sem.at[0],
            recv_sem=near_sem.at[1],
            device_id=column_peer(k),
            device_id_type=MESH,
        ).start()

    for load in loads[4:]:
        load.wait()
    rows_n = table_v.shape[0]
    lanes = acc_v.shape[1]
    touched_row = touched_v[...]
    eye = iota((slots_n, slots_n), 0) == iota((slots_n, slots_n), 1)

    def to_column(line):
        return jnp.sum(jnp.where(eye, line, 0.0), axis=1, keepdims=True)

    touched_col = to_column(touched_row.astype(F32)).astype(jnp.int32)
    pick = (iota((slots_n, rows_n), 1) == touched_col).astype(F32).astype(BF16)
    old_rows = dot_nn(pick, table_v[...])
    gain = gain_v[...]
    w_out = w_out_v[...]
    width = w_out.shape[1]
    pre_act = dot_nn(old_rows.astype(BF16), w_in_v[...])
    sig_pre = jax.nn.sigmoid(pre_act)
    hidden = pre_act * sig_pre
    inv_rms = lax.rsqrt(jnp.sum(hidden * hidden, axis=1, keepdims=True) * (1.0 / width) + 1e-06)
    mixed = dot_nn((hidden * inv_rms * gain).astype(BF16), w_mid_v[...])
    sig_mix = jax.nn.sigmoid(mixed)
    logits = jnp.sum((hidden + mixed * sig_mix) * w_out, axis=1, keepdims=True)
    click = jax.nn.sigmoid(logits)
    d_mixed = (w_out * silu_slope(mixed, sig_mix)).astype(BF16)

    pltpu.make_async_copy(near_recv, near_recv, near_sem.at[1]).wait()
    column = both(z)
    for slot in range(UP + REACH):
        column = column + near_recv[slot]
    for x_i in range(N_XHI):
        plane_send[x_i] = column[x_i * 2 : x_i * 2 + 2, :]
    mine = rep * N_XHI + x_hi
    for xhi_i, peer in plane_peers:
        pltpu.make_async_remote_copy(
            src_ref=plane_send.at[xhi_i],
            dst_ref=plane_recv.at[mine],
            send_sem=plane_sem.at[0],
            recv_sem=plane_sem.at[1],
            device_id=peer,
            device_id_type=MESH,
        ).start()
    plane_recv[mine] = plane_send[x_hi]

    gained = dot_nt(d_mixed, w_mid_v[...]) * gain
    dotted = jnp.sum(hidden * gained, axis=1, keepdims=True) * (1.0 / width)
    d_hidden = w_out + inv_rms * gained - hidden * (inv_rms * inv_rms * inv_rms * dotted)
    d_pre = (d_hidden * silu_slope(pre_act, sig_pre)).astype(BF16)
    unit_grad = dot_nt(d_pre, w_in_v[...])

    lo_col = lax.rem(touched_col, lanes)
    hi_col = lax.div(touched_col, lanes)
    acc_rows = acc_v.shape[0]
    hi_hot = (iota((slots_n, acc_rows), 1) == hi_col).astype(F32).astype(BF16)
    lo_hit = iota((slots_n, lanes), 1) == lo_col
    acc_parts = [dot_nn(hi_hot, piece) for piece in split3(acc_v[...])]
    acc_lines = acc_parts[0] + acc_parts[1] + acc_parts[2]
    old_acc = jnp.sum(jnp.where(lo_hit, acc_lines, 0.0), axis=1, keepdims=True)
    hi_hot_t = (
        (iota((acc_rows, slots_n), 0) == lax.div(touched_row, lanes)).astype(F32).astype(BF16)
    )
    acc_hit = dot_nn(hi_hot_t, lo_hit.astype(F32).astype(BF16)) > 0.5

    place = (iota((rows_n, slots_n), 0) == touched_row).astype(F32).astype(BF16)
    place_ref[...] = place
    hits = dot_nn(place, jnp.ones((slots_n, table_v.shape[1]), BF16))
    rest_ref[...] = jnp.where(hits > 0.5, 0.0, table_v[...].astype(F32)).astype(BF16)

    n_p = len(plane_peers)
    pltpu.make_async_copy(
        plane_recv.at[pl.ds(0, n_p)], plane_recv.at[pl.ds(0, n_p)], plane_sem.at[1]
    ).wait()
    total = plane_recv[0]
    for i in range(1, n_p + 1):
        total = total + plane_recv[i]

    d_sum = to_column(total[0:1, :]) * click - to_column(total[1:2, :])
    grad = d_sum * unit_grad
    acc_new = old_acc + jnp.sum(grad * grad, axis=1, keepdims=True)
    rows_ref[...] = (old_rows - learn_rate * grad * lax.rsqrt(acc_new)).astype(BF16)
    spread = jnp.where(lo_hit, acc_new, 0.0)
    placed = [dot_nn(hi_hot_t, piece) for piece in split3(spread)]
    acc_out_ref[...] = jnp.where(acc_hit, placed[0] + placed[1] + placed[2], acc_v[...])

    core_copy.wait_send()
    pltpu.make_async_copy(far_recv, far_recv, far_sent).wait()
    pltpu.make_async_copy(near_recv, near_recv, near_sem.at[0]).wait()
    pltpu.make_async_copy(
        plane_recv.at[pl.ds(0, n_p)], plane_recv.at[pl.ds(0, n_p)], plane_sem.at[0]
    ).wait()


def scatter_kernel(rows_ref, acc_ref, place_ref, rest_ref, table_out, acc_out, tiles, sem):
    acc_copy = pltpu.make_async_copy(acc_ref, acc_out, sem.at[0])
    acc_copy.start()
    rows = rows_ref[...]
    count = tiles.shape[0]
    step = tiles.shape[1]
    copies = []
    for i in range(count):
        span = slice(i * step, (i + 1) * step)
        tiles[i] = (dot_nn(place_ref[span, :], rows) + rest_ref[span, :].astype(F32)).astype(BF16)
        copy = pltpu.make_async_copy(tiles.at[i], table_out.at[pl.ds(i * step, step)], sem.at[i + 1])
        copy.start()
        copies.append(copy)
    for copy in copies:
        copy.wait()
    acc_copy.wait()


def on_device(
    n_y,
    n_z,
    owner_shard,
    slot_index,
    lengths,
    labels,
    embed_table,
    accumulator,
    touched,
    w_in,
    w_mid,
    norm_gain,
    w_out,
):
    rows_n, emb = embed_table.shape
    slots_n = touched.shape[0]
    width = w_out.shape[0]
    lanes = 128
    acc2 = accumulator.reshape(rows_n // lanes, lanes)
    touched2 = touched.reshape(1, slots_n)
    hbm_spec = pl.BlockSpec(memory_space=pltpu.HBM)
    vmem = pl.BlockSpec(memory_space=pltpu.VMEM)
    n_far = UP + DOWN
    n_near = UP + REACH
    part = N_XHI * 2
    operands = [
        pltpu.with_memory_space_constraint(array, pltpu.HBM)
        for array in (
            owner_shard,
            slot_index,
            lengths,
            labels,
            embed_table,
            acc2,
            touched2,
            w_in,
            w_mid,
            norm_gain.reshape(1, width),
            w_out.reshape(1, width),
        )
    ]
    made = pl.pallas_call(
        functools.partial(reduce_kernel, n_y, n_z),
        out_shape=(
            jax.ShapeDtypeStruct((slots_n, emb), BF16),
            jax.ShapeDtypeStruct(acc2.shape, F32),
            jax.ShapeDtypeStruct((rows_n, slots_n), BF16),
            jax.ShapeDtypeStruct((rows_n, emb), BF16),
        ),
        in_specs=[hbm_spec] * len(operands),
        out_specs=(vmem,) * 4,
        scratch_shapes=[
            pltpu.VMEM(owner_shard.shape, jnp.int32),
            pltpu.VMEM(slot_index.shape, jnp.int32),
            pltpu.SMEM(lengths.shape, jnp.int32),
            pltpu.VMEM(labels.shape, F32),
            pltpu.VMEM(embed_table.shape, BF16),
            pltpu.VMEM(acc2.shape, F32),
            pltpu.VMEM(touched2.shape, jnp.int32),
            pltpu.VMEM(w_in.shape, BF16),
            pltpu.VMEM(w_mid.shape, BF16),
            pltpu.VMEM((1, width), F32),
            pltpu.VMEM((1, width), F32),
            pltpu.SemaphoreType.DMA((11,)),
            pltpu.VMEM((N_CORE * n_z, part, slots_n), F32),
            pltpu.VMEM((n_far, N_CORE, part, slots_n), F32),
            pltpu.VMEM((n_near, part, slots_n), F32),
            pltpu.VMEM((n_near, part, slots_n), F32),
            pltpu.VMEM((n_z, part, slots_n), F32),
            pltpu.VMEM((N_XHI, 2, slots_n), F32),
            pltpu.VMEM((N_XHI * n_y * N_XLO, 2, slots_n), F32),
            pltpu.SemaphoreType.DMA((n_far,)),
            pltpu.SemaphoreType.DMA,
            pltpu.SemaphoreType.DMA((2,)),
            pltpu.SemaphoreType.DMA((2,)),
            pltpu.SemaphoreType.DMA((2,)),
        ],
        compiler_params=pltpu.CompilerParams(
            collective_id=0, has_side_effects=True, vmem_limit_bytes=32 * 1024 * 1024
        ),
        name="reduce",
    )(*operands)
    tiles = 4
    table_out, accum_out = pl.pallas_call(
        scatter_kernel,
        out_shape=(
            jax.ShapeDtypeStruct(embed_table.shape, BF16),
            jax.ShapeDtypeStruct(acc2.shape, F32),
        ),
        in_specs=[vmem] * 4,
        out_specs=(hbm_spec,) * 2,
        scratch_shapes=[
            pltpu.VMEM((tiles, rows_n // tiles, emb), BF16),
            pltpu.SemaphoreType.DMA((tiles + 1,)),
        ],
        compiler_params=pltpu.CompilerParams(vmem_limit_bytes=24 * 1024 * 1024),
        name="scatter",
    )(*made)
    return (table_out, accum_out.reshape(rows_n))


def solution(mesh):
    n_y = mesh.shape["replica"] // N_XLO
    n_z = mesh.shape["mp"] // (N_CORE * N_XHI)
    in_specs = (
        P(("replica", "mp"), None),
        P(("replica", "mp"), None),
        P(("replica", "mp")),
        P(("replica", "mp"), None),
        P("mp", None),
        P("mp"),
        P("mp"),
        P(),
        P(),
        P(),
        P(),
    )
    out_specs = (P("mp", None), P("mp"))
    return jax.shard_map(
        functools.partial(on_device, n_y, n_z),
        mesh=mesh,
        in_specs=in_specs,
        out_specs=out_specs,
        check_vma=False,
    )
```

```python
import functools

import jax
import jax.numpy as jnp
from jax import lax
from jax.experimental import pallas as pl
from jax.experimental.pallas import tpu as pltpu
from jax.sharding import PartitionSpec as P

MESH = pl.DeviceIdType.MESH
F32 = jnp.float32
BF16 = jnp.bfloat16
learn_rate = 1.0

N_CORE = 2
N_XHI = 2
N_XLO = 2
REACH = 4
UP = REACH
DOWN = REACH - 1


def split3(values):
    high = values.astype(BF16)
    rest = values - high.astype(F32)
    mid = rest.astype(BF16)
    low = (rest - mid.astype(F32)).astype(BF16)
    return high, mid, low


def dot_nn(a, b):
    return jnp.dot(a, b, preferred_element_type=F32)


def dot_nt(a, b):
    return lax.dot_general(a, b, (((1,), (1,)), ((), ())), preferred_element_type=F32)


def silu_slope(values, sigma_val):
    return sigma_val * (1.0 + values * (1.0 - sigma_val))


def iota(shape, dim):
    return lax.broadcasted_iota(jnp.int32, shape, dim)


def ring(size, shift):
    return min(shift % size, -shift % size)


def reduce_kernel(
    n_y,
    n_z,
    owner_hbm,
    slot_hbm,
    len_hbm,
    label_hbm,
    table_hbm,
    acc_hbm,
    touched_hbm,
    w_in_hbm,
    w_mid_hbm,
    gain_hbm,
    w_out_hbm,
    rows_ref,
    acc_ref,
    place_ref,
    rest_ref,
    hi_hot_ref,
    acc_rest_ref,
    owner_v,
    slot_v,
    len_s,
    label_v,
    table_v,
    acc_v,
    touched_v,
    w_in_v,
    w_mid_v,
    gain_v,
    w_out_v,
    in_sem,
    hist,
    far_recv,
    near_send,
    near_recv,
    core_recv,
    plane_send,
    plane_recv,
    far_sems,
    far_sent,
    near_sem,
    core_sem,
    plane_sem,
):
    rep = lax.axis_index("replica")
    mp = lax.axis_index("mp")
    core = lax.rem(mp, N_CORE)
    x_hi = lax.rem(lax.div(mp, N_CORE), N_XHI)
    z = lax.div(mp, N_CORE * N_XHI)
    y = lax.div(rep, N_XLO)
    n_x = N_XHI * N_XLO
    x = x_hi * N_XLO + lax.rem(rep, N_XLO)

    def column_peer(shift, turn=0):
        z_i = lax.rem(z + (shift + n_z), n_z)
        return (rep, (z_i * N_XHI + x_hi) * N_CORE + lax.rem(core + turn, N_CORE))

    def block(shift):
        return lax.rem(z + (shift + 2 * n_z), n_z)

    plane = [(dy, dx) for dy in range(n_y) for dx in range(n_x) if (dy, dx) != (0, 0)]
    plane.sort(key=lambda d: -(ring(n_y, d[0]) + ring(n_x, d[1])))
    plane_peers = []
    for dy, dx in plane:
        y_i, x_i = lax.rem(y + dy, n_y), lax.rem(x + dx, n_x)
        xhi_i = lax.div(x_i, N_XLO)
        rep_i = y_i * N_XLO + lax.rem(x_i, N_XLO)
        plane_peers.append((xhi_i, (rep_i, (z * N_XHI + xhi_i) * N_CORE + core)))
    partner = (rep, mp + 1 - 2 * core)
    shifts = [s for k in range(REACH, 0, -1) for s in (k, -k)]

    sources = [
        (owner_hbm, owner_v),
        (slot_hbm, slot_v),
        (label_hbm, label_v),
        (len_hbm, len_s),
        (touched_hbm, touched_v),
        (table_hbm, table_v),
        (w_in_hbm, w_in_v),
        (w_mid_hbm, w_mid_v),
        (gain_hbm, gain_v),
        (w_out_hbm, w_out_v),
        (acc_hbm, acc_v),
    ]
    loads = [
        pltpu.make_async_copy(src, dst, in_sem.at[i]) for i, (src, dst) in enumerate(sources)
    ]
    barrier = pltpu.get_barrier_semaphore()
    greeted = (
        [column_peer(hop, turn) for turn in range(N_CORE) for hop in (REACH, -REACH)]
        + [column_peer(shift) for shift in shifts if abs(shift) != REACH]
        + [peer for _, peer in plane_peers]
        + [partner]
    )
    for peer in greeted:
        pl.semaphore_signal(barrier, inc=1, device_id=peer, device_id_type=MESH)
    for load in loads[:4]:
        load.start()
    for load in loads[4:]:
        load.start()

    samples, length = owner_v.shape
    part = hist.shape[1]
    n_rows = hist.shape[0] * part
    slots_n = hist.shape[2]
    row = iota((n_rows, slots_n), 0)
    counts = lax.rem(row, 2) == 0
    row_z = lax.rem(lax.div(row, part), n_z)
    row_x = lax.rem(lax.div(row, 2), N_XHI)
    row_owner = (row_z * N_XHI + row_x) * N_CORE + lax.div(row, n_z * part)
    slot_iota = iota((slots_n, slots_n), 0)
    lane = iota((1, slots_n), 1)
    for load in loads[:4]:
        load.wait()
    parts, hots = [[], [], []], []
    for sample in range(samples):
        for start in range(0, length, slots_n):
            window = (slice(sample, sample + 1), slice(start, start + slots_n))
            live = (lane + start < len_s[sample]).astype(F32)
            high, mid, low = (live * part.astype(F32) for part in split3(label_v[window]))
            hit = row_owner == owner_v[window]
            labelled = hit & ~counts
            parts[0].append(jnp.where(hit, jnp.where(counts, live, high), 0.0).astype(BF16))
            parts[1].append(jnp.where(labelled, mid, 0.0).astype(BF16))
            parts[2].append(jnp.where(labelled, low, 0.0).astype(BF16))
            hots.append((slot_iota == slot_v[window]).astype(F32).astype(BF16))
    stacked = jnp.concatenate([jnp.concatenate(part, axis=1) for part in parts], axis=0)
    counted = dot_nt(stacked, jnp.concatenate(hots, axis=1))
    counted = counted[:n_rows] + counted[n_rows : 2 * n_rows] + counted[2 * n_rows :]
    for i in range(N_CORE * n_z):
        hist[i] = counted[i * part : (i + 1) * part, :]

    pl.semaphore_wait(barrier, len(greeted))

    core_copy = pltpu.make_async_remote_copy(
        src_ref=hist.at[pl.ds((1 - core) * n_z, n_z)],
        dst_ref=core_recv,
        send_sem=core_sem.at[0],
        recv_sem=core_sem.at[1],
        device_id=partner,
        device_id_type=MESH,
    )
    core_copy.start()

    def slot_of(k):
        return k - 1 if k > 0 else UP - k - 1

    order = [s for s in shifts if s != -REACH]
    for k in order:
        hop = REACH if k > 0 else -REACH
        for turn in (1, 0):
            pltpu.make_async_remote_copy(
                src_ref=hist.at[lax.rem(core + turn, N_CORE) * n_z + block(hop + k)],
                dst_ref=far_recv.at[slot_of(k), core],
                send_sem=far_sent,
                recv_sem=far_sems.at[slot_of(k)],
                device_id=column_peer(hop, turn),
                device_id_type=MESH,
            ).start()

    core_copy.wait_recv()

    def both(z_i):
        return hist[core * n_z + z_i] + core_recv[z_i]

    for k in [-REACH] + order:
        slot = slot_of(k)
        own = both(block(k))
        if k != -REACH:
            arrived = far_recv.at[slot]
            pltpu.make_async_copy(arrived, arrived, far_sems.at[slot]).wait()
            own = own + (far_recv[slot, 0] + far_recv[slot, 1])
        near_send[slot] = own
        pltpu.make_async_remote_copy(
            src_ref=near_send.at[slot],
            dst_ref=near_recv.at[slot],
            send_sem=near_sem.at[0],
            recv_sem=near_sem.at[1],
            device_id=column_peer(k),
            device_id_type=MESH,
        ).start()

    for load in loads[4:]:
        load.wait()
    rows_n = table_v.shape[0]
    lanes = acc_v.shape[1]
    touched_row = touched_v[...]
    eye = iota((slots_n, slots_n), 0) == iota((slots_n, slots_n), 1)

    def to_column(line):
        return jnp.sum(jnp.where(eye, line, 0.0), axis=1, keepdims=True)

    touched_col = to_column(touched_row.astype(F32)).astype(jnp.int32)
    pick = (iota((slots_n, rows_n), 1) == touched_col).astype(F32).astype(BF16)
    old_rows = dot_nn(pick, table_v[...])
    gain = gain_v[...]
    w_out = w_out_v[...]
    width = w_out.shape[1]
    pre_act = dot_nn(old_rows.astype(BF16), w_in_v[...])
    sig_pre = jax.nn.sigmoid(pre_act)
    hidden = pre_act * sig_pre
    inv_rms = lax.rsqrt(jnp.sum(hidden * hidden, axis=1, keepdims=True) * (1.0 / width) + 1e-06)
    mixed = dot_nn((hidden * inv_rms * gain).astype(BF16), w_mid_v[...])
    sig_mix = jax.nn.sigmoid(mixed)
    logits = jnp.sum((hidden + mixed * sig_mix) * w_out, axis=1, keepdims=True)
    click = jax.nn.sigmoid(logits)
    d_mixed = (w_out * silu_slope(mixed, sig_mix)).astype(BF16)

    pltpu.make_async_copy(near_recv, near_recv, near_sem.at[1]).wait()
    column = both(z)
    for slot in range(UP + REACH):
        column = column + near_recv[slot]
    for x_i in range(N_XHI):
        plane_send[x_i] = column[x_i * 2 : x_i * 2 + 2, :]
    mine = rep * N_XHI + x_hi
    for xhi_i, peer in plane_peers:
        pltpu.make_async_remote_copy(
            src_ref=plane_send.at[xhi_i],
            dst_ref=plane_recv.at[mine],
            send_sem=plane_sem.at[0],
            recv_sem=plane_sem.at[1],
            device_id=peer,
            device_id_type=MESH,
        ).start()
    plane_recv[mine] = plane_send[x_hi]

    gained = dot_nt(d_mixed, w_mid_v[...]) * gain
    dotted = jnp.sum(hidden * gained, axis=1, keepdims=True) * (1.0 / width)
    d_hidden = w_out + inv_rms * gained - hidden * (inv_rms * inv_rms * inv_rms * dotted)
    d_pre = (d_hidden * silu_slope(pre_act, sig_pre)).astype(BF16)
    unit_grad = dot_nt(d_pre, w_in_v[...])
    unit_square = jnp.sum(unit_grad * unit_grad, axis=1, keepdims=True)

    lo_col = lax.rem(touched_col, lanes)
    hi_col = lax.div(touched_col, lanes)
    acc_rows = acc_v.shape[0]
    hi_hot = (iota((slots_n, acc_rows), 1) == hi_col).astype(F32).astype(BF16)
    lo_hit = iota((slots_n, lanes), 1) == lo_col
    acc_parts = [dot_nn(hi_hot, piece) for piece in split3(acc_v[...])]
    acc_lines = acc_parts[0] + acc_parts[1] + acc_parts[2]
    old_acc = jnp.sum(jnp.where(lo_hit, acc_lines, 0.0), axis=1, keepdims=True)
    hi_hot_t = (
        (iota((acc_rows, slots_n), 0) == lax.div(touched_row, lanes)).astype(F32).astype(BF16)
    )
    hi_hot_ref[...] = hi_hot_t
    acc_hit = dot_nn(hi_hot_t, lo_hit.astype(F32).astype(BF16)) > 0.5
    acc_rest_ref[...] = jnp.where(acc_hit, 0.0, acc_v[...])

    place = (iota((rows_n, slots_n), 0) == touched_row).astype(F32).astype(BF16)
    place_ref[...] = place
    hits = dot_nn(place, jnp.ones((slots_n, table_v.shape[1]), BF16))
    rest_ref[...] = jnp.where(hits > 0.5, 0.0, table_v[...].astype(F32)).astype(BF16)

    n_p = len(plane_peers)
    pltpu.make_async_copy(
        plane_recv.at[pl.ds(0, n_p)], plane_recv.at[pl.ds(0, n_p)], plane_sem.at[1]
    ).wait()
    total = plane_recv[0]
    for i in range(1, n_p + 1):
        total = total + plane_recv[i]

    d_sum = to_column(total[0:1, :]) * click - to_column(total[1:2, :])
    acc_new = old_acc + d_sum * d_sum * unit_square
    rows_ref[...] = (old_rows - (learn_rate * d_sum * lax.rsqrt(acc_new)) * unit_grad).astype(BF16)
    acc_ref[...] = jnp.where(lo_hit, acc_new, 0.0)

    core_copy.wait_send()
    pltpu.make_async_copy(far_recv, far_recv, far_sent).wait()
    pltpu.make_async_copy(near_recv, near_recv, near_sem.at[0]).wait()
    pltpu.make_async_copy(
        plane_recv.at[pl.ds(0, n_p)], plane_recv.at[pl.ds(0, n_p)], plane_sem.at[0]
    ).wait()


def scatter_kernel(
    rows_ref, acc_ref, place_ref, rest_ref, hi_hot_ref, acc_rest_ref, table_out, acc_out, tiles, acc_tile, sem
):
    rows = rows_ref[...]
    count = tiles.shape[0]
    step = tiles.shape[1]
    copies = []
    for i in range(count):
        span = slice(i * step, (i + 1) * step)
        tiles[i] = (dot_nn(place_ref[span, :], rows) + rest_ref[span, :].astype(F32)).astype(BF16)
        copies.append(
            pltpu.make_async_copy(tiles.at[i], table_out.at[pl.ds(i * step, step)], sem.at[i + 1])
        )
        copies[-1].start()
        if i == count - 2:
            placed = [dot_nn(hi_hot_ref[...], piece) for piece in split3(acc_ref[...])]
            acc_tile[...] = acc_rest_ref[...] + (placed[0] + placed[1] + placed[2])
            copies.append(pltpu.make_async_copy(acc_tile, acc_out, sem.at[0]))
            copies[-1].start()
    for copy in copies:
        copy.wait()


def on_device(
    n_y,
    n_z,
    owner_shard,
    slot_index,
    lengths,
    labels,
    embed_table,
    accumulator,
    touched,
    w_in,
    w_mid,
    norm_gain,
    w_out,
):
    rows_n, emb = embed_table.shape
    slots_n = touched.shape[0]
    width = w_out.shape[0]
    lanes = 128
    acc2 = accumulator.reshape(rows_n // lanes, lanes)
    touched2 = touched.reshape(1, slots_n)
    hbm_spec = pl.BlockSpec(memory_space=pltpu.HBM)
    vmem = pl.BlockSpec(memory_space=pltpu.VMEM)
    n_far = UP + DOWN
    n_near = UP + REACH
    part = N_XHI * 2
    operands = [
        pltpu.with_memory_space_constraint(array, pltpu.HBM)
        for array in (
            owner_shard,
            slot_index,
            lengths,
            labels,
            embed_table,
            acc2,
            touched2,
            w_in,
            w_mid,
            norm_gain.reshape(1, width),
            w_out.reshape(1, width),
        )
    ]
    made = pl.pallas_call(
        functools.partial(reduce_kernel, n_y, n_z),
        out_shape=(
            jax.ShapeDtypeStruct((slots_n, emb), BF16),
            jax.ShapeDtypeStruct((slots_n, lanes), F32),
            jax.ShapeDtypeStruct((rows_n, slots_n), BF16),
            jax.ShapeDtypeStruct((rows_n, emb), BF16),
            jax.ShapeDtypeStruct((acc2.shape[0], slots_n), BF16),
            jax.ShapeDtypeStruct(acc2.shape, F32),
        ),
        in_specs=[hbm_spec] * len(operands),
        out_specs=(vmem,) * 6,
        scratch_shapes=[
            pltpu.VMEM(owner_shard.shape, jnp.int32),
            pltpu.VMEM(slot_index.shape, jnp.int32),
            pltpu.SMEM(lengths.shape, jnp.int32),
            pltpu.VMEM(labels.shape, F32),
            pltpu.VMEM(embed_table.shape, BF16),
            pltpu.VMEM(acc2.shape, F32),
            pltpu.VMEM(touched2.shape, jnp.int32),
            pltpu.VMEM(w_in.shape, BF16),
            pltpu.VMEM(w_mid.shape, BF16),
            pltpu.VMEM((1, width), F32),
            pltpu.VMEM((1, width), F32),
            pltpu.SemaphoreType.DMA((11,)),
            pltpu.VMEM((N_CORE * n_z, part, slots_n), F32),
            pltpu.VMEM((n_far, N_CORE, part, slots_n), F32),
            pltpu.VMEM((n_near, part, slots_n), F32),
            pltpu.VMEM((n_near, part, slots_n), F32),
            pltpu.VMEM((n_z, part, slots_n), F32),
            pltpu.VMEM((N_XHI, 2, slots_n), F32),
            pltpu.VMEM((N_XHI * n_y * N_XLO, 2, slots_n), F32),
            pltpu.SemaphoreType.DMA((n_far,)),
            pltpu.SemaphoreType.DMA,
            pltpu.SemaphoreType.DMA((2,)),
            pltpu.SemaphoreType.DMA((2,)),
            pltpu.SemaphoreType.DMA((2,)),
        ],
        compiler_params=pltpu.CompilerParams(
            collective_id=0, has_side_effects=True, vmem_limit_bytes=32 * 1024 * 1024
        ),
        name="reduce",
    )(*operands)
    tiles = 4
    table_out, accum_out = pl.pallas_call(
        scatter_kernel,
        out_shape=(
            jax.ShapeDtypeStruct(embed_table.shape, BF16),
            jax.ShapeDtypeStruct(acc2.shape, F32),
        ),
        in_specs=[vmem] * 6,
        out_specs=(hbm_spec,) * 2,
        scratch_shapes=[
            pltpu.VMEM((tiles, rows_n // tiles, emb), BF16),
            pltpu.VMEM(acc2.shape, F32),
            pltpu.SemaphoreType.DMA((tiles + 1,)),
        ],
        compiler_params=pltpu.CompilerParams(vmem_limit_bytes=24 * 1024 * 1024),
        name="scatter",
    )(*made)
    return (table_out, accum_out.reshape(rows_n))


def solution(mesh):
    n_y = mesh.shape["replica"] // N_XLO
    n_z = mesh.shape["mp"] // (N_CORE * N_XHI)
    in_specs = (
        P(("replica", "mp"), None),
        P(("replica", "mp"), None),
        P(("replica", "mp")),
        P(("replica", "mp"), None),
        P("mp", None),
        P("mp"),
        P("mp"),
        P(),
        P(),
        P(),
        P(),
    )
    out_specs = (P("mp", None), P("mp"))
    return jax.shard_map(
        functools.partial(on_device, n_y, n_z),
        mesh=mesh,
        in_specs=in_specs,
        out_specs=out_specs,
        check_vma=False,
    )
```

```python
import functools

import jax
import jax.numpy as jnp
from jax import lax
from jax.experimental import pallas as pl
from jax.experimental.pallas import tpu as pltpu
from jax.sharding import PartitionSpec as P

MESH = pl.DeviceIdType.MESH
F32 = jnp.float32
BF16 = jnp.bfloat16
learn_rate = 1.0

N_CORE = 2
N_XHI = 2
N_XLO = 2
REACH = 4
UP = REACH
DOWN = REACH - 1


def split3(values):
    high = values.astype(BF16)
    rest = values - high.astype(F32)
    mid = rest.astype(BF16)
    low = (rest - mid.astype(F32)).astype(BF16)
    return high, mid, low


def dot_nn(a, b):
    return jnp.dot(a, b, preferred_element_type=F32)


def dot_nt(a, b):
    return lax.dot_general(a, b, (((1,), (1,)), ((), ())), preferred_element_type=F32)


def tree_sum(terms):
    while len(terms) > 1:
        pairs = [a + b for a, b in zip(terms[::2], terms[1::2])]
        terms = pairs + terms[2 * len(pairs) :]
    return terms[0]


def silu_slope(values, sigma_val):
    return sigma_val * (1.0 + values * (1.0 - sigma_val))


def iota(shape, dim):
    return lax.broadcasted_iota(jnp.int32, shape, dim)


def ring(size, shift):
    return min(shift % size, -shift % size)


def reduce_kernel(
    n_y,
    n_z,
    owner_hbm,
    slot_hbm,
    len_hbm,
    label_hbm,
    table_hbm,
    acc_hbm,
    touched_hbm,
    w_in_hbm,
    w_mid_hbm,
    gain_hbm,
    w_out_hbm,
    rows_ref,
    acc_ref,
    place_ref,
    rest_ref,
    hi_hot_ref,
    acc_rest_ref,
    owner_v,
    slot_v,
    len_s,
    label_v,
    table_v,
    acc_v,
    touched_v,
    w_in_v,
    w_mid_v,
    gain_v,
    w_out_v,
    in_sem,
    hist,
    far_recv,
    near_send,
    near_recv,
    core_recv,
    plane_send,
    plane_recv,
    far_sems,
    far_sent,
    near_sem,
    core_sem,
    plane_sem,
):
    rep = lax.axis_index("replica")
    mp = lax.axis_index("mp")
    core = lax.rem(mp, N_CORE)
    x_hi = lax.rem(lax.div(mp, N_CORE), N_XHI)
    z = lax.div(mp, N_CORE * N_XHI)
    y = lax.div(rep, N_XLO)
    n_x = N_XHI * N_XLO
    x = x_hi * N_XLO + lax.rem(rep, N_XLO)

    def column_peer(shift, turn=0):
        z_i = lax.rem(z + (shift + n_z), n_z)
        return (rep, (z_i * N_XHI + x_hi) * N_CORE + lax.rem(core + turn, N_CORE))

    def block(shift):
        return lax.rem(z + (shift + 2 * n_z), n_z)

    plane = [(dy, dx) for dy in range(n_y) for dx in range(n_x) if (dy, dx) != (0, 0)]
    plane.sort(key=lambda d: -(ring(n_y, d[0]) + ring(n_x, d[1])))
    plane_peers = []
    for dy, dx in plane:
        y_i, x_i = lax.rem(y + dy, n_y), lax.rem(x + dx, n_x)
        xhi_i = lax.div(x_i, N_XLO)
        rep_i = y_i * N_XLO + lax.rem(x_i, N_XLO)
        plane_peers.append((xhi_i, (rep_i, (z * N_XHI + xhi_i) * N_CORE + core)))
    partner = (rep, mp + 1 - 2 * core)
    shifts = [s for k in range(REACH, 0, -1) for s in (k, -k)]

    sources = [
        (owner_hbm, owner_v),
        (slot_hbm, slot_v),
        (label_hbm, label_v),
        (len_hbm, len_s),
        (touched_hbm, touched_v),
        (table_hbm, table_v),
        (w_in_hbm, w_in_v),
        (w_mid_hbm, w_mid_v),
        (gain_hbm, gain_v),
        (w_out_hbm, w_out_v),
        (acc_hbm, acc_v),
    ]
    loads = [
        pltpu.make_async_copy(src, dst, in_sem.at[i]) for i, (src, dst) in enumerate(sources)
    ]
    barrier = pltpu.get_barrier_semaphore()
    greeted = (
        [column_peer(hop, turn) for turn in range(N_CORE) for hop in (REACH, -REACH)]
        + [column_peer(shift) for shift in shifts if abs(shift) != REACH]
        + [peer for _, peer in plane_peers]
        + [partner]
    )
    for peer in greeted:
        pl.semaphore_signal(barrier, inc=1, device_id=peer, device_id_type=MESH)
    for load in loads[:4]:
        load.start()
    for load in loads[4:]:
        load.start()

    samples, length = owner_v.shape
    part = hist.shape[1]
    n_rows = hist.shape[0] * part
    slots_n = hist.shape[2]
    row = iota((n_rows, slots_n), 0)
    counts = lax.rem(row, 2) == 0
    row_z = lax.rem(lax.div(row, part), n_z)
    row_x = lax.rem(lax.div(row, 2), N_XHI)
    row_owner = (row_z * N_XHI + row_x) * N_CORE + lax.div(row, n_z * part)
    slot_iota = iota((slots_n, slots_n), 0)
    lane = iota((1, slots_n), 1)
    for load in loads[:4]:
        load.wait()
    parts, hots = [[], [], []], []
    for sample in range(samples):
        for start in range(0, length, slots_n):
            window = (slice(sample, sample + 1), slice(start, start + slots_n))
            live = (lane + start < len_s[sample]).astype(F32)
            high, mid, low = (live * part.astype(F32) for part in split3(label_v[window]))
            hit = row_owner == owner_v[window]
            labelled = hit & ~counts
            parts[0].append(jnp.where(hit, jnp.where(counts, live, high), 0.0).astype(BF16))
            parts[1].append(jnp.where(labelled, mid, 0.0).astype(BF16))
            parts[2].append(jnp.where(labelled, low, 0.0).astype(BF16))
            hots.append((slot_iota == slot_v[window]).astype(F32).astype(BF16))
    stacked = jnp.concatenate([jnp.concatenate(part, axis=1) for part in parts], axis=0)
    counted = dot_nt(stacked, jnp.concatenate(hots, axis=1))
    counted = counted[:n_rows] + counted[n_rows : 2 * n_rows] + counted[2 * n_rows :]
    for i in range(N_CORE * n_z):
        hist[i] = counted[i * part : (i + 1) * part, :]

    pl.semaphore_wait(barrier, len(greeted))

    core_copy = pltpu.make_async_remote_copy(
        src_ref=hist.at[pl.ds((1 - core) * n_z, n_z)],
        dst_ref=core_recv,
        send_sem=core_sem.at[0],
        recv_sem=core_sem.at[1],
        device_id=partner,
        device_id_type=MESH,
    )
    core_copy.start()

    def slot_of(k):
        return k - 1 if k > 0 else UP - k - 1

    order = [s for s in shifts if s != -REACH]
    for k in order:
        hop = REACH if k > 0 else -REACH
        for turn in (1, 0):
            pltpu.make_async_remote_copy(
                src_ref=hist.at[lax.rem(core + turn, N_CORE) * n_z + block(hop + k)],
                dst_ref=far_recv.at[slot_of(k), core],
                send_sem=far_sent,
                recv_sem=far_sems.at[slot_of(k)],
                device_id=column_peer(hop, turn),
                device_id_type=MESH,
            ).start()

    core_copy.wait_recv()

    def both(z_i):
        return hist[core * n_z + z_i] + core_recv[z_i]

    for k in [-REACH] + order:
        slot = slot_of(k)
        own = both(block(k))
        if k != -REACH:
            arrived = far_recv.at[slot]
            pltpu.make_async_copy(arrived, arrived, far_sems.at[slot]).wait()
            own = own + (far_recv[slot, 0] + far_recv[slot, 1])
        near_send[slot] = own
        pltpu.make_async_remote_copy(
            src_ref=near_send.at[slot],
            dst_ref=near_recv.at[slot],
            send_sem=near_sem.at[0],
            recv_sem=near_sem.at[1],
            device_id=column_peer(k),
            device_id_type=MESH,
        ).start()

    for load in loads[4:]:
        load.wait()
    rows_n = table_v.shape[0]
    lanes = acc_v.shape[1]
    touched_row = touched_v[...]
    eye = iota((slots_n, slots_n), 0) == iota((slots_n, slots_n), 1)

    def to_column(line):
        return jnp.sum(jnp.where(eye, line, 0.0), axis=1, keepdims=True)

    touched_col = to_column(touched_row.astype(F32)).astype(jnp.int32)
    pick = (iota((slots_n, rows_n), 1) == touched_col).astype(F32).astype(BF16)
    old_rows = dot_nn(pick, table_v[...])
    gain = gain_v[...]
    w_out = w_out_v[...]
    width = w_out.shape[1]
    pre_act = dot_nn(old_rows.astype(BF16), w_in_v[...])
    sig_pre = jax.nn.sigmoid(pre_act)
    hidden = pre_act * sig_pre
    inv_rms = lax.rsqrt(jnp.sum(hidden * hidden, axis=1, keepdims=True) * (1.0 / width) + 1e-06)
    mixed = dot_nn((hidden * inv_rms * gain).astype(BF16), w_mid_v[...])
    sig_mix = jax.nn.sigmoid(mixed)
    logits = jnp.sum((hidden + mixed * sig_mix) * w_out, axis=1, keepdims=True)
    click_row = jnp.sum(jnp.where(eye, jax.nn.sigmoid(logits), 0.0), axis=0, keepdims=True)
    d_mixed = (w_out * silu_slope(mixed, sig_mix)).astype(BF16)

    pltpu.make_async_copy(near_recv, near_recv, near_sem.at[1]).wait()
    column = tree_sum([both(z)] + [near_recv[slot] for slot in range(UP + REACH)])
    for x_i in range(N_XHI):
        plane_send[x_i] = column[x_i * 2 : x_i * 2 + 2, :]
    mine = rep * N_XHI + x_hi
    for xhi_i, peer in plane_peers:
        pltpu.make_async_remote_copy(
            src_ref=plane_send.at[xhi_i],
            dst_ref=plane_recv.at[mine],
            send_sem=plane_sem.at[0],
            recv_sem=plane_sem.at[1],
            device_id=peer,
            device_id_type=MESH,
        ).start()
    plane_recv[mine] = plane_send[x_hi]

    gained = dot_nt(d_mixed, w_mid_v[...]) * gain
    dotted = jnp.sum(hidden * gained, axis=1, keepdims=True) * (1.0 / width)
    d_hidden = w_out + inv_rms * gained - hidden * (inv_rms * inv_rms * inv_rms * dotted)
    d_pre = (d_hidden * silu_slope(pre_act, sig_pre)).astype(BF16)
    unit_grad = dot_nt(d_pre, w_in_v[...])
    unit_square = jnp.sum(unit_grad * unit_grad, axis=1, keepdims=True)

    lo_col = lax.rem(touched_col, lanes)
    hi_col = lax.div(touched_col, lanes)
    acc_rows = acc_v.shape[0]
    hi_hot = (iota((slots_n, acc_rows), 1) == hi_col).astype(F32).astype(BF16)
    lo_hit = iota((slots_n, lanes), 1) == lo_col
    acc_parts = [dot_nn(hi_hot, piece) for piece in split3(acc_v[...])]
    acc_lines = acc_parts[0] + acc_parts[1] + acc_parts[2]
    old_acc = jnp.sum(jnp.where(lo_hit, acc_lines, 0.0), axis=1, keepdims=True)
    hi_hot_t = (
        (iota((acc_rows, slots_n), 0) == lax.div(touched_row, lanes)).astype(F32).astype(BF16)
    )
    hi_hot_ref[...] = hi_hot_t
    acc_hit = dot_nn(hi_hot_t, lo_hit.astype(F32).astype(BF16)) > 0.5
    acc_rest_ref[...] = jnp.where(acc_hit, 0.0, acc_v[...])

    place = (iota((rows_n, slots_n), 0) == touched_row).astype(F32).astype(BF16)
    place_ref[...] = place
    hits = dot_nn(place, jnp.ones((slots_n, table_v.shape[1]), BF16))
    rest_ref[...] = jnp.where(hits > 0.5, 0.0, table_v[...].astype(F32)).astype(BF16)

    n_p = len(plane_peers)
    pltpu.make_async_copy(
        plane_recv.at[pl.ds(0, n_p)], plane_recv.at[pl.ds(0, n_p)], plane_sem.at[1]
    ).wait()
    total = tree_sum([plane_recv[i] for i in range(n_p + 1)])

    d_sum = to_column(total[0:1, :] * click_row - total[1:2, :])
    acc_new = old_acc + d_sum * d_sum * unit_square
    rows_ref[...] = (old_rows - (learn_rate * d_sum * lax.rsqrt(acc_new)) * unit_grad).astype(BF16)
    acc_ref[...] = jnp.where(lo_hit, acc_new, 0.0)

    core_copy.wait_send()
    pltpu.make_async_copy(far_recv, far_recv, far_sent).wait()
    pltpu.make_async_copy(near_recv, near_recv, near_sem.at[0]).wait()
    pltpu.make_async_copy(
        plane_recv.at[pl.ds(0, n_p)], plane_recv.at[pl.ds(0, n_p)], plane_sem.at[0]
    ).wait()


def scatter_kernel(
    rows_ref, acc_ref, place_ref, rest_ref, hi_hot_ref, acc_rest_ref, table_out, acc_out, tiles, acc_tile, sem
):
    rows = rows_ref[...]
    count = tiles.shape[0]
    step = tiles.shape[1]
    copies = []
    for i in range(count):
        span = slice(i * step, (i + 1) * step)
        tiles[i] = (dot_nn(place_ref[span, :], rows) + rest_ref[span, :].astype(F32)).astype(BF16)
        copies.append(
            pltpu.make_async_copy(tiles.at[i], table_out.at[pl.ds(i * step, step)], sem.at[i + 1])
        )
        copies[-1].start()
        if i == count - 2:
            placed = [dot_nn(hi_hot_ref[...], piece) for piece in split3(acc_ref[...])]
            acc_tile[...] = acc_rest_ref[...] + (placed[0] + placed[1] + placed[2])
            copies.append(pltpu.make_async_copy(acc_tile, acc_out, sem.at[0]))
            copies[-1].start()
    for copy in copies:
        copy.wait()


def on_device(
    n_y,
    n_z,
    owner_shard,
    slot_index,
    lengths,
    labels,
    embed_table,
    accumulator,
    touched,
    w_in,
    w_mid,
    norm_gain,
    w_out,
):
    rows_n, emb = embed_table.shape
    slots_n = touched.shape[0]
    width = w_out.shape[0]
    lanes = 128
    acc2 = accumulator.reshape(rows_n // lanes, lanes)
    touched2 = touched.reshape(1, slots_n)
    hbm_spec = pl.BlockSpec(memory_space=pltpu.HBM)
    vmem = pl.BlockSpec(memory_space=pltpu.VMEM)
    n_far = UP + DOWN
    n_near = UP + REACH
    part = N_XHI * 2
    operands = [
        pltpu.with_memory_space_constraint(array, pltpu.HBM)
        for array in (
            owner_shard,
            slot_index,
            lengths,
            labels,
            embed_table,
            acc2,
            touched2,
            w_in,
            w_mid,
            norm_gain.reshape(1, width),
            w_out.reshape(1, width),
        )
    ]
    made = pl.pallas_call(
        functools.partial(reduce_kernel, n_y, n_z),
        out_shape=(
            jax.ShapeDtypeStruct((slots_n, emb), BF16),
            jax.ShapeDtypeStruct((slots_n, lanes), F32),
            jax.ShapeDtypeStruct((rows_n, slots_n), BF16),
            jax.ShapeDtypeStruct((rows_n, emb), BF16),
            jax.ShapeDtypeStruct((acc2.shape[0], slots_n), BF16),
            jax.ShapeDtypeStruct(acc2.shape, F32),
        ),
        in_specs=[hbm_spec] * len(operands),
        out_specs=(vmem,) * 6,
        scratch_shapes=[
            pltpu.VMEM(owner_shard.shape, jnp.int32),
            pltpu.VMEM(slot_index.shape, jnp.int32),
            pltpu.SMEM(lengths.shape, jnp.int32),
            pltpu.VMEM(labels.shape, F32),
            pltpu.VMEM(embed_table.shape, BF16),
            pltpu.VMEM(acc2.shape, F32),
            pltpu.VMEM(touched2.shape, jnp.int32),
            pltpu.VMEM(w_in.shape, BF16),
            pltpu.VMEM(w_mid.shape, BF16),
            pltpu.VMEM((1, width), F32),
            pltpu.VMEM((1, width), F32),
            pltpu.SemaphoreType.DMA((11,)),
            pltpu.VMEM((N_CORE * n_z, part, slots_n), F32),
            pltpu.VMEM((n_far, N_CORE, part, slots_n), F32),
            pltpu.VMEM((n_near, part, slots_n), F32),
            pltpu.VMEM((n_near, part, slots_n), F32),
            pltpu.VMEM((n_z, part, slots_n), F32),
            pltpu.VMEM((N_XHI, 2, slots_n), F32),
            pltpu.VMEM((N_XHI * n_y * N_XLO, 2, slots_n), F32),
            pltpu.SemaphoreType.DMA((n_far,)),
            pltpu.SemaphoreType.DMA,
            pltpu.SemaphoreType.DMA((2,)),
            pltpu.SemaphoreType.DMA((2,)),
            pltpu.SemaphoreType.DMA((2,)),
        ],
        compiler_params=pltpu.CompilerParams(
            collective_id=0, has_side_effects=True, vmem_limit_bytes=32 * 1024 * 1024
        ),
        name="reduce",
    )(*operands)
    tiles = 4
    table_out, accum_out = pl.pallas_call(
        scatter_kernel,
        out_shape=(
            jax.ShapeDtypeStruct(embed_table.shape, BF16),
            jax.ShapeDtypeStruct(acc2.shape, F32),
        ),
        in_specs=[vmem] * 6,
        out_specs=(hbm_spec,) * 2,
        scratch_shapes=[
            pltpu.VMEM((tiles, rows_n // tiles, emb), BF16),
            pltpu.VMEM(acc2.shape, F32),
            pltpu.SemaphoreType.DMA((tiles + 1,)),
        ],
        compiler_params=pltpu.CompilerParams(vmem_limit_bytes=24 * 1024 * 1024),
        name="scatter",
    )(*made)
    return (table_out, accum_out.reshape(rows_n))


def solution(mesh):
    n_y = mesh.shape["replica"] // N_XLO
    n_z = mesh.shape["mp"] // (N_CORE * N_XHI)
    in_specs = (
        P(("replica", "mp"), None),
        P(("replica", "mp"), None),
        P(("replica", "mp")),
        P(("replica", "mp"), None),
        P("mp", None),
        P("mp"),
        P("mp"),
        P(),
        P(),
        P(),
        P(),
    )
    out_specs = (P("mp", None), P("mp"))
    return jax.shard_map(
        functools.partial(on_device, n_y, n_z),
        mesh=mesh,
        in_specs=in_specs,
        out_specs=out_specs,
        check_vma=False,
    )
```

```python
import functools

import jax
import jax.numpy as jnp
from jax import lax
from jax.experimental import pallas as pl
from jax.experimental.pallas import tpu as pltpu
from jax.sharding import PartitionSpec as P

MESH = pl.DeviceIdType.MESH
F32 = jnp.float32
BF16 = jnp.bfloat16
learn_rate = 1.0

N_CORE = 2
N_XHI = 2
N_XLO = 2
REACH = 4
UP = REACH
DOWN = REACH - 1


def split3(values):
    high = values.astype(BF16)
    rest = values - high.astype(F32)
    mid = rest.astype(BF16)
    low = (rest - mid.astype(F32)).astype(BF16)
    return high, mid, low


def dot_nn(a, b):
    return jnp.dot(a, b, preferred_element_type=F32)


def dot_nt(a, b):
    return lax.dot_general(a, b, (((1,), (1,)), ((), ())), preferred_element_type=F32)


def tree_sum(terms):
    while len(terms) > 1:
        pairs = [a + b for a, b in zip(terms[::2], terms[1::2])]
        terms = pairs + terms[2 * len(pairs) :]
    return terms[0]


def silu_slope(values, sigma_val):
    return sigma_val * (1.0 + values * (1.0 - sigma_val))


def iota(shape, dim):
    return lax.broadcasted_iota(jnp.int32, shape, dim)


def ring(size, shift):
    return min(shift % size, -shift % size)


def reduce_kernel(
    n_y,
    n_z,
    owner_hbm,
    slot_hbm,
    len_hbm,
    label_hbm,
    table_hbm,
    acc_hbm,
    touched_hbm,
    w_in_hbm,
    w_mid_hbm,
    gain_hbm,
    w_out_hbm,
    rows_ref,
    acc_ref,
    place_ref,
    rest_ref,
    hi_hot_ref,
    acc_rest_ref,
    owner_v,
    slot_v,
    len_s,
    label_v,
    table_v,
    acc_v,
    touched_v,
    w_in_v,
    w_mid_v,
    gain_v,
    w_out_v,
    in_sem,
    hist,
    far_recv,
    near_send,
    near_recv,
    core_recv,
    plane_send,
    plane_recv,
    far_sems,
    far_sent,
    near_sem,
    core_sem,
    plane_sem,
):
    rep = lax.axis_index("replica")
    mp = lax.axis_index("mp")
    core = lax.rem(mp, N_CORE)
    x_hi = lax.rem(lax.div(mp, N_CORE), N_XHI)
    z = lax.div(mp, N_CORE * N_XHI)
    y = lax.div(rep, N_XLO)
    n_x = N_XHI * N_XLO
    x = x_hi * N_XLO + lax.rem(rep, N_XLO)

    def column_peer(shift, turn=0):
        z_i = lax.rem(z + (shift + n_z), n_z)
        return (rep, (z_i * N_XHI + x_hi) * N_CORE + lax.rem(core + turn, N_CORE))

    def block(shift):
        return lax.rem(z + (shift + 2 * n_z), n_z)

    plane = [(dy, dx) for dy in range(n_y) for dx in range(n_x) if (dy, dx) != (0, 0)]
    plane.sort(key=lambda d: -(ring(n_y, d[0]) + ring(n_x, d[1])))
    plane_peers = []
    for dy, dx in plane:
        y_i, x_i = lax.rem(y + dy, n_y), lax.rem(x + dx, n_x)
        xhi_i = lax.div(x_i, N_XLO)
        rep_i = y_i * N_XLO + lax.rem(x_i, N_XLO)
        plane_peers.append((xhi_i, (rep_i, (z * N_XHI + xhi_i) * N_CORE + core)))
    partner = (rep, mp + 1 - 2 * core)
    shifts = [s for k in range(REACH, 0, -1) for s in (k, -k)]

    sources = [
        (owner_hbm, owner_v),
        (slot_hbm, slot_v),
        (label_hbm, label_v),
        (len_hbm, len_s),
        (touched_hbm, touched_v),
        (table_hbm, table_v),
        (w_in_hbm, w_in_v),
        (w_mid_hbm, w_mid_v),
        (gain_hbm, gain_v),
        (w_out_hbm, w_out_v),
        (acc_hbm, acc_v),
    ]
    loads = [
        pltpu.make_async_copy(src, dst, in_sem.at[i]) for i, (src, dst) in enumerate(sources)
    ]
    barrier = pltpu.get_barrier_semaphore()
    greeted = (
        [column_peer(hop, turn) for turn in range(N_CORE) for hop in (REACH, -REACH)]
        + [column_peer(shift) for shift in shifts if abs(shift) != REACH]
        + [peer for _, peer in plane_peers]
        + [partner]
    )
    for peer in greeted:
        pl.semaphore_signal(barrier, inc=1, device_id=peer, device_id_type=MESH)
    for load in loads[:4]:
        load.start()
    for load in loads[4:]:
        load.start()

    samples, length = owner_v.shape
    part = hist.shape[1]
    n_rows = hist.shape[0] * part
    slots_n = hist.shape[2]
    row = iota((n_rows, slots_n), 0)
    counts = lax.rem(row, 2) == 0
    row_z = lax.rem(lax.div(row, part), n_z)
    row_x = lax.rem(lax.div(row, 2), N_XHI)
    row_owner = (row_z * N_XHI + row_x) * N_CORE + lax.div(row, n_z * part)
    slot_iota = iota((slots_n, slots_n), 0)
    lane = iota((1, slots_n), 1)
    for load in loads[:4]:
        load.wait()
    parts, hots = [[], [], []], []
    for sample in range(samples):
        for start in range(0, length, slots_n):
            window = (slice(sample, sample + 1), slice(start, start + slots_n))
            live = (lane + start < len_s[sample]).astype(F32)
            high, mid, low = (live * part.astype(F32) for part in split3(label_v[window]))
            hit = row_owner == owner_v[window]
            labelled = hit & ~counts
            parts[0].append(jnp.where(hit, jnp.where(counts, live, high), 0.0).astype(BF16))
            parts[1].append(jnp.where(labelled, mid, 0.0).astype(BF16))
            parts[2].append(jnp.where(labelled, low, 0.0).astype(BF16))
            hots.append((slot_iota == slot_v[window]).astype(F32).astype(BF16))
    stacked = jnp.concatenate([jnp.concatenate(part, axis=1) for part in parts], axis=0)
    counted = dot_nt(stacked, jnp.concatenate(hots, axis=1))
    counted = counted[:n_rows] + counted[n_rows : 2 * n_rows] + counted[2 * n_rows :]
    for i in range(N_CORE * n_z):
        hist[i] = counted[i * part : (i + 1) * part, :]

    pl.semaphore_wait(barrier, len(greeted))

    core_copy = pltpu.make_async_remote_copy(
        src_ref=hist.at[pl.ds((1 - core) * n_z, n_z)],
        dst_ref=core_recv,
        send_sem=core_sem.at[0],
        recv_sem=core_sem.at[1],
        device_id=partner,
        device_id_type=MESH,
    )
    core_copy.start()

    def slot_of(k):
        return k - 1 if k > 0 else UP - k - 1

    order = [s for s in shifts if s != -REACH]
    for k in order:
        hop = REACH if k > 0 else -REACH
        for turn in (1, 0):
            pltpu.make_async_remote_copy(
                src_ref=hist.at[lax.rem(core + turn, N_CORE) * n_z + block(hop + k)],
                dst_ref=far_recv.at[slot_of(k), core],
                send_sem=far_sent,
                recv_sem=far_sems.at[slot_of(k)],
                device_id=column_peer(hop, turn),
                device_id_type=MESH,
            ).start()

    core_copy.wait_recv()

    def both(z_i):
        return hist[core * n_z + z_i] + core_recv[z_i]

    for k in [-REACH] + order:
        slot = slot_of(k)
        own = both(block(k))
        if k != -REACH:
            arrived = far_recv.at[slot]
            pltpu.make_async_copy(arrived, arrived, far_sems.at[slot]).wait()
            own = own + (far_recv[slot, 0] + far_recv[slot, 1])
        near_send[slot] = own
        pltpu.make_async_remote_copy(
            src_ref=near_send.at[slot],
            dst_ref=near_recv.at[slot],
            send_sem=near_sem.at[0],
            recv_sem=near_sem.at[1],
            device_id=column_peer(k),
            device_id_type=MESH,
        ).start()

    for load in loads[4:]:
        load.wait()
    rows_n = table_v.shape[0]
    lanes = acc_v.shape[1]
    touched_row = touched_v[...]
    eye = iota((slots_n, slots_n), 0) == iota((slots_n, slots_n), 1)

    def to_column(line):
        return jnp.sum(jnp.where(eye, line, 0.0), axis=1, keepdims=True)

    touched_col = to_column(touched_row.astype(F32)).astype(jnp.int32)
    pick = (iota((slots_n, rows_n), 1) == touched_col).astype(F32).astype(BF16)
    old_rows = dot_nn(pick, table_v[...])
    gain = gain_v[...]
    w_out = w_out_v[...]
    width = w_out.shape[1]
    pre_act = dot_nn(old_rows.astype(BF16), w_in_v[...])
    sig_pre = jax.nn.sigmoid(pre_act)
    hidden = pre_act * sig_pre
    inv_rms = lax.rsqrt(jnp.sum(hidden * hidden, axis=1, keepdims=True) * (1.0 / width) + 1e-06)
    mixed = dot_nn((hidden * inv_rms * gain).astype(BF16), w_mid_v[...])
    sig_mix = jax.nn.sigmoid(mixed)
    logits = jnp.sum((hidden + mixed * sig_mix) * w_out, axis=1, keepdims=True)
    click_row = jnp.sum(jnp.where(eye, jax.nn.sigmoid(logits), 0.0), axis=0, keepdims=True)
    d_mixed = (w_out * silu_slope(mixed, sig_mix)).astype(BF16)

    pltpu.make_async_copy(near_recv, near_recv, near_sem.at[1]).wait()
    column = tree_sum([both(z)] + [near_recv[slot] for slot in range(UP + REACH)])
    for x_i in range(N_XHI):
        plane_send[x_i] = column[x_i * 2 : x_i * 2 + 2, :]
    mine = rep * N_XHI + x_hi
    for xhi_i, peer in plane_peers:
        pltpu.make_async_remote_copy(
            src_ref=plane_send.at[xhi_i],
            dst_ref=plane_recv.at[mine],
            send_sem=plane_sem.at[0],
            recv_sem=plane_sem.at[1],
            device_id=peer,
            device_id_type=MESH,
        ).start()
    plane_recv[mine] = plane_send[x_hi]

    gained = dot_nt(d_mixed, w_mid_v[...]) * gain
    dotted = jnp.sum(hidden * gained, axis=1, keepdims=True) * (1.0 / width)
    d_hidden = w_out + inv_rms * gained - hidden * (inv_rms * inv_rms * inv_rms * dotted)
    d_pre = (d_hidden * silu_slope(pre_act, sig_pre)).astype(BF16)
    unit_grad = dot_nt(d_pre, w_in_v[...])
    unit_square = jnp.sum(unit_grad * unit_grad, axis=1, keepdims=True)

    lo_col = lax.rem(touched_col, lanes)
    hi_col = lax.div(touched_col, lanes)
    acc_rows = acc_v.shape[0]
    hi_hot = (iota((slots_n, acc_rows), 1) == hi_col).astype(F32).astype(BF16)
    lo_hit = iota((slots_n, lanes), 1) == lo_col
    acc_parts = [dot_nn(hi_hot, piece) for piece in split3(acc_v[...])]
    acc_lines = acc_parts[0] + acc_parts[1] + acc_parts[2]
    old_acc = jnp.sum(jnp.where(lo_hit, acc_lines, 0.0), axis=1, keepdims=True)
    hi_hot_t = (
        (iota((acc_rows, slots_n), 0) == lax.div(touched_row, lanes)).astype(F32).astype(BF16)
    )
    hi_hot_ref[...] = hi_hot_t
    acc_hit = dot_nn(hi_hot_t, lo_hit.astype(F32).astype(BF16)) > 0.5
    acc_rest_ref[...] = jnp.where(acc_hit, 0.0, acc_v[...])

    place = (iota((rows_n, slots_n), 0) == touched_row).astype(F32).astype(BF16)
    place_ref[...] = place
    hits = dot_nn(place, jnp.ones((slots_n, table_v.shape[1]), BF16))
    rest_ref[...] = jnp.where(hits > 0.5, 0.0, table_v[...].astype(F32)).astype(BF16)

    n_p = len(plane_peers)
    pltpu.make_async_copy(
        plane_recv.at[pl.ds(0, n_p)], plane_recv.at[pl.ds(0, n_p)], plane_sem.at[1]
    ).wait()
    total = tree_sum([plane_recv[i] for i in range(n_p + 1)])

    d_sum = to_column(total[0:1, :] * click_row - total[1:2, :])
    acc_new = old_acc + d_sum * d_sum * unit_square
    rows_ref[...] = (old_rows - (learn_rate * d_sum * lax.rsqrt(acc_new)) * unit_grad).astype(BF16)
    acc_ref[...] = jnp.where(lo_hit, acc_new, 0.0)

    core_copy.wait_send()
    pltpu.make_async_copy(far_recv, far_recv, far_sent).wait()
    pltpu.make_async_copy(near_recv, near_recv, near_sem.at[0]).wait()
    pltpu.make_async_copy(
        plane_recv.at[pl.ds(0, n_p)], plane_recv.at[pl.ds(0, n_p)], plane_sem.at[0]
    ).wait()


def scatter_kernel(
    rows_ref, acc_ref, place_ref, rest_ref, hi_hot_ref, acc_rest_ref, table_out, acc_out, tiles, acc_tile, sem
):
    rows = rows_ref[...]
    count = tiles.shape[0]
    step = tiles.shape[1]
    copies = []
    for i in range(count):
        span = slice(i * step, (i + 1) * step)
        tiles[i] = (dot_nn(place_ref[span, :], rows) + rest_ref[span, :].astype(F32)).astype(BF16)
        copies.append(
            pltpu.make_async_copy(tiles.at[i], table_out.at[pl.ds(i * step, step)], sem.at[i + 1])
        )
        copies[-1].start()
        if i == count - 1:
            placed = [dot_nn(hi_hot_ref[...], piece) for piece in split3(acc_ref[...])]
            acc_tile[...] = acc_rest_ref[...] + (placed[0] + placed[1] + placed[2])
            copies.append(pltpu.make_async_copy(acc_tile, acc_out, sem.at[0]))
            copies[-1].start()
    for copy in copies:
        copy.wait()


def on_device(
    n_y,
    n_z,
    owner_shard,
    slot_index,
    lengths,
    labels,
    embed_table,
    accumulator,
    touched,
    w_in,
    w_mid,
    norm_gain,
    w_out,
):
    rows_n, emb = embed_table.shape
    slots_n = touched.shape[0]
    width = w_out.shape[0]
    lanes = 128
    acc2 = accumulator.reshape(rows_n // lanes, lanes)
    touched2 = touched.reshape(1, slots_n)
    hbm_spec = pl.BlockSpec(memory_space=pltpu.HBM)
    vmem = pl.BlockSpec(memory_space=pltpu.VMEM)
    n_far = UP + DOWN
    n_near = UP + REACH
    part = N_XHI * 2
    operands = [
        pltpu.with_memory_space_constraint(array, pltpu.HBM)
        for array in (
            owner_shard,
            slot_index,
            lengths,
            labels,
            embed_table,
            acc2,
            touched2,
            w_in,
            w_mid,
            norm_gain.reshape(1, width),
            w_out.reshape(1, width),
        )
    ]
    made = pl.pallas_call(
        functools.partial(reduce_kernel, n_y, n_z),
        out_shape=(
            jax.ShapeDtypeStruct((slots_n, emb), BF16),
            jax.ShapeDtypeStruct((slots_n, lanes), F32),
            jax.ShapeDtypeStruct((rows_n, slots_n), BF16),
            jax.ShapeDtypeStruct((rows_n, emb), BF16),
            jax.ShapeDtypeStruct((acc2.shape[0], slots_n), BF16),
            jax.ShapeDtypeStruct(acc2.shape, F32),
        ),
        in_specs=[hbm_spec] * len(operands),
        out_specs=(vmem,) * 6,
        scratch_shapes=[
            pltpu.VMEM(owner_shard.shape, jnp.int32),
            pltpu.VMEM(slot_index.shape, jnp.int32),
            pltpu.SMEM(lengths.shape, jnp.int32),
            pltpu.VMEM(labels.shape, F32),
            pltpu.VMEM(embed_table.shape, BF16),
            pltpu.VMEM(acc2.shape, F32),
            pltpu.VMEM(touched2.shape, jnp.int32),
            pltpu.VMEM(w_in.shape, BF16),
            pltpu.VMEM(w_mid.shape, BF16),
            pltpu.VMEM((1, width), F32),
            pltpu.VMEM((1, width), F32),
            pltpu.SemaphoreType.DMA((11,)),
            pltpu.VMEM((N_CORE * n_z, part, slots_n), F32),
            pltpu.VMEM((n_far, N_CORE, part, slots_n), F32),
            pltpu.VMEM((n_near, part, slots_n), F32),
            pltpu.VMEM((n_near, part, slots_n), F32),
            pltpu.VMEM((n_z, part, slots_n), F32),
            pltpu.VMEM((N_XHI, 2, slots_n), F32),
            pltpu.VMEM((N_XHI * n_y * N_XLO, 2, slots_n), F32),
            pltpu.SemaphoreType.DMA((n_far,)),
            pltpu.SemaphoreType.DMA,
            pltpu.SemaphoreType.DMA((2,)),
            pltpu.SemaphoreType.DMA((2,)),
            pltpu.SemaphoreType.DMA((2,)),
        ],
        compiler_params=pltpu.CompilerParams(
            collective_id=0, has_side_effects=True, vmem_limit_bytes=32 * 1024 * 1024
        ),
        name="reduce",
    )(*operands)
    tiles = 4
    table_out, accum_out = pl.pallas_call(
        scatter_kernel,
        out_shape=(
            jax.ShapeDtypeStruct(embed_table.shape, BF16),
            jax.ShapeDtypeStruct(acc2.shape, F32),
        ),
        in_specs=[vmem] * 6,
        out_specs=(hbm_spec,) * 2,
        scratch_shapes=[
            pltpu.VMEM((tiles, rows_n // tiles, emb), BF16),
            pltpu.VMEM(acc2.shape, F32),
            pltpu.SemaphoreType.DMA((tiles + 1,)),
        ],
        compiler_params=pltpu.CompilerParams(vmem_limit_bytes=24 * 1024 * 1024),
        name="scatter",
    )(*made)
    return (table_out, accum_out.reshape(rows_n))


def solution(mesh):
    n_y = mesh.shape["replica"] // N_XLO
    n_z = mesh.shape["mp"] // (N_CORE * N_XHI)
    in_specs = (
        P(("replica", "mp"), None),
        P(("replica", "mp"), None),
        P(("replica", "mp")),
        P(("replica", "mp"), None),
        P("mp", None),
        P("mp"),
        P("mp"),
        P(),
        P(),
        P(),
        P(),
    )
    out_specs = (P("mp", None), P("mp"))
    return jax.shard_map(
        functools.partial(on_device, n_y, n_z),
        mesh=mesh,
        in_specs=in_specs,
        out_specs=out_specs,
        check_vma=False,
    )
```

```python
import functools

import jax
import jax.numpy as jnp
from jax import lax
from jax.experimental import pallas as pl
from jax.experimental.pallas import tpu as pltpu
from jax.sharding import PartitionSpec as P

MESH = pl.DeviceIdType.MESH
F32 = jnp.float32
BF16 = jnp.bfloat16
learn_rate = 1.0

N_CORE = 2
N_XHI = 2
N_XLO = 2
REACH = 4
UP = REACH
DOWN = REACH - 1


def split3(values):
    high = values.astype(BF16)
    rest = values - high.astype(F32)
    mid = rest.astype(BF16)
    low = (rest - mid.astype(F32)).astype(BF16)
    return high, mid, low


def dot_nn(a, b):
    return jnp.dot(a, b, preferred_element_type=F32)


def dot_nt(a, b):
    return lax.dot_general(a, b, (((1,), (1,)), ((), ())), preferred_element_type=F32)


def tree_sum(terms):
    while len(terms) > 1:
        pairs = [a + b for a, b in zip(terms[::2], terms[1::2])]
        terms = pairs + terms[2 * len(pairs) :]
    return terms[0]


def silu_slope(values, sigma_val):
    return sigma_val * (1.0 + values * (1.0 - sigma_val))


def iota(shape, dim):
    return lax.broadcasted_iota(jnp.int32, shape, dim)


def ring(size, shift):
    return min(shift % size, -shift % size)


def reduce_kernel(
    n_y,
    n_z,
    owner_hbm,
    slot_hbm,
    len_hbm,
    label_hbm,
    table_hbm,
    acc_hbm,
    touched_hbm,
    w_in_hbm,
    w_mid_hbm,
    gain_hbm,
    w_out_hbm,
    rows_ref,
    acc_ref,
    place_ref,
    rest_ref,
    hi_hot_ref,
    acc_rest_ref,
    owner_v,
    slot_v,
    len_s,
    label_v,
    table_v,
    acc_v,
    touched_v,
    w_in_v,
    w_mid_v,
    gain_v,
    w_out_v,
    in_sem,
    hist,
    far_recv,
    near_send,
    near_recv,
    core_recv,
    plane_send,
    plane_recv,
    far_sems,
    far_sent,
    near_sem,
    core_sem,
    plane_sem,
):
    rep = lax.axis_index("replica")
    mp = lax.axis_index("mp")
    core = lax.rem(mp, N_CORE)
    x_hi = lax.rem(lax.div(mp, N_CORE), N_XHI)
    z = lax.div(mp, N_CORE * N_XHI)
    y = lax.div(rep, N_XLO)
    n_x = N_XHI * N_XLO
    x = x_hi * N_XLO + lax.rem(rep, N_XLO)

    def column_peer(shift, turn=0):
        z_i = lax.rem(z + (shift + n_z), n_z)
        return (rep, (z_i * N_XHI + x_hi) * N_CORE + lax.rem(core + turn, N_CORE))

    def block(shift):
        return lax.rem(z + (shift + 2 * n_z), n_z)

    plane = [(dy, dx) for dy in range(n_y) for dx in range(n_x) if (dy, dx) != (0, 0)]
    plane.sort(key=lambda d: -(ring(n_y, d[0]) + ring(n_x, d[1])))
    plane_peers = []
    for dy, dx in plane:
        y_i, x_i = lax.rem(y + dy, n_y), lax.rem(x + dx, n_x)
        xhi_i = lax.div(x_i, N_XLO)
        rep_i = y_i * N_XLO + lax.rem(x_i, N_XLO)
        plane_peers.append((xhi_i, (rep_i, (z * N_XHI + xhi_i) * N_CORE + core)))
    partner = (rep, mp + 1 - 2 * core)
    shifts = [s for k in range(REACH, 0, -1) for s in (k, -k)]

    sources = [
        (owner_hbm, owner_v),
        (slot_hbm, slot_v),
        (label_hbm, label_v),
        (len_hbm, len_s),
        (touched_hbm, touched_v),
        (table_hbm, table_v),
        (w_in_hbm, w_in_v),
        (w_mid_hbm, w_mid_v),
        (gain_hbm, gain_v),
        (w_out_hbm, w_out_v),
        (acc_hbm, acc_v),
    ]
    loads = [
        pltpu.make_async_copy(src, dst, in_sem.at[i]) for i, (src, dst) in enumerate(sources)
    ]
    barrier = pltpu.get_barrier_semaphore()
    greeted = (
        [column_peer(hop, turn) for turn in range(N_CORE) for hop in (REACH, -REACH)]
        + [column_peer(shift) for shift in shifts if abs(shift) != REACH]
        + [peer for _, peer in plane_peers]
        + [partner]
    )
    for peer in greeted:
        pl.semaphore_signal(barrier, inc=1, device_id=peer, device_id_type=MESH)
    for load in loads[:4]:
        load.start()
    for load in loads[4:]:
        load.start()

    samples, length = owner_v.shape
    part = hist.shape[1]
    n_rows = hist.shape[0] * part
    slots_n = hist.shape[2]
    row = iota((n_rows, slots_n), 0)
    counts = lax.rem(row, 2) == 0
    row_z = lax.rem(lax.div(row, part), n_z)
    row_x = lax.rem(lax.div(row, 2), N_XHI)
    row_owner = (row_z * N_XHI + row_x) * N_CORE + lax.div(row, n_z * part)
    slot_iota = iota((slots_n, slots_n), 0)
    lane = iota((1, slots_n), 1)
    for load in loads[:4]:
        load.wait()
    parts, hots = [[], [], []], []
    for sample in range(samples):
        for start in range(0, length, slots_n):
            window = (slice(sample, sample + 1), slice(start, start + slots_n))
            live = (lane + start < len_s[sample]).astype(F32)
            high, mid, low = (live * part.astype(F32) for part in split3(label_v[window]))
            hit = row_owner == owner_v[window]
            labelled = hit & ~counts
            parts[0].append(jnp.where(hit, jnp.where(counts, live, high), 0.0).astype(BF16))
            parts[1].append(jnp.where(labelled, mid, 0.0).astype(BF16))
            parts[2].append(jnp.where(labelled, low, 0.0).astype(BF16))
            hots.append((slot_iota == slot_v[window]).astype(F32).astype(BF16))
    stacked = jnp.concatenate([jnp.concatenate(part, axis=1) for part in parts], axis=0)
    counted = dot_nt(stacked, jnp.concatenate(hots, axis=1))
    counted = counted[:n_rows] + counted[n_rows : 2 * n_rows] + counted[2 * n_rows :]
    for i in range(N_CORE * n_z):
        hist[i] = counted[i * part : (i + 1) * part, :]

    pl.semaphore_wait(barrier, len(greeted))

    core_copy = pltpu.make_async_remote_copy(
        src_ref=hist.at[pl.ds((1 - core) * n_z, n_z)],
        dst_ref=core_recv,
        send_sem=core_sem.at[0],
        recv_sem=core_sem.at[1],
        device_id=partner,
        device_id_type=MESH,
    )

    def slot_of(k):
        return k - 1 if k > 0 else UP - k - 1

    order = [s for s in shifts if s != -REACH]
    for k in order:
        hop = REACH if k > 0 else -REACH
        for turn in (1, 0):
            pltpu.make_async_remote_copy(
                src_ref=hist.at[lax.rem(core + turn, N_CORE) * n_z + block(hop + k)],
                dst_ref=far_recv.at[slot_of(k), core],
                send_sem=far_sent,
                recv_sem=far_sems.at[slot_of(k)],
                device_id=column_peer(hop, turn),
                device_id_type=MESH,
            ).start()

    core_copy.start()

    core_copy.wait_recv()

    def both(z_i):
        return hist[core * n_z + z_i] + core_recv[z_i]

    for k in [-REACH] + order:
        slot = slot_of(k)
        own = both(block(k))
        if k != -REACH:
            arrived = far_recv.at[slot]
            pltpu.make_async_copy(arrived, arrived, far_sems.at[slot]).wait()
            own = own + (far_recv[slot, 0] + far_recv[slot, 1])
        near_send[slot] = own
        pltpu.make_async_remote_copy(
            src_ref=near_send.at[slot],
            dst_ref=near_recv.at[slot],
            send_sem=near_sem.at[0],
            recv_sem=near_sem.at[1],
            device_id=column_peer(k),
            device_id_type=MESH,
        ).start()

    for load in loads[4:]:
        load.wait()
    rows_n = table_v.shape[0]
    lanes = acc_v.shape[1]
    touched_row = touched_v[...]
    eye = iota((slots_n, slots_n), 0) == iota((slots_n, slots_n), 1)

    def to_column(line):
        return jnp.sum(jnp.where(eye, line, 0.0), axis=1, keepdims=True)

    touched_col = to_column(touched_row.astype(F32)).astype(jnp.int32)
    pick = (iota((slots_n, rows_n), 1) == touched_col).astype(F32).astype(BF16)
    old_rows = dot_nn(pick, table_v[...])
    gain = gain_v[...]
    w_out = w_out_v[...]
    width = w_out.shape[1]
    pre_act = dot_nn(old_rows.astype(BF16), w_in_v[...])
    sig_pre = jax.nn.sigmoid(pre_act)
    hidden = pre_act * sig_pre
    inv_rms = lax.rsqrt(jnp.sum(hidden * hidden, axis=1, keepdims=True) * (1.0 / width) + 1e-06)
    mixed = dot_nn((hidden * inv_rms * gain).astype(BF16), w_mid_v[...])
    sig_mix = jax.nn.sigmoid(mixed)
    logits = jnp.sum((hidden + mixed * sig_mix) * w_out, axis=1, keepdims=True)
    click_row = jnp.sum(jnp.where(eye, jax.nn.sigmoid(logits), 0.0), axis=0, keepdims=True)
    d_mixed = (w_out * silu_slope(mixed, sig_mix)).astype(BF16)

    pltpu.make_async_copy(near_recv, near_recv, near_sem.at[1]).wait()
    column = tree_sum([both(z)] + [near_recv[slot] for slot in range(UP + REACH)])
    for x_i in range(N_XHI):
        plane_send[x_i] = column[x_i * 2 : x_i * 2 + 2, :]
    mine = rep * N_XHI + x_hi
    for xhi_i, peer in plane_peers:
        pltpu.make_async_remote_copy(
            src_ref=plane_send.at[xhi_i],
            dst_ref=plane_recv.at[mine],
            send_sem=plane_sem.at[0],
            recv_sem=plane_sem.at[1],
            device_id=peer,
            device_id_type=MESH,
        ).start()
    plane_recv[mine] = plane_send[x_hi]

    gained = dot_nt(d_mixed, w_mid_v[...]) * gain
    dotted = jnp.sum(hidden * gained, axis=1, keepdims=True) * (1.0 / width)
    d_hidden = w_out + inv_rms * gained - hidden * (inv_rms * inv_rms * inv_rms * dotted)
    d_pre = (d_hidden * silu_slope(pre_act, sig_pre)).astype(BF16)
    unit_grad = dot_nt(d_pre, w_in_v[...])
    unit_square = jnp.sum(unit_grad * unit_grad, axis=1, keepdims=True)

    lo_col = lax.rem(touched_col, lanes)
    hi_col = lax.div(touched_col, lanes)
    acc_rows = acc_v.shape[0]
    hi_hot = (iota((slots_n, acc_rows), 1) == hi_col).astype(F32).astype(BF16)
    lo_hit = iota((slots_n, lanes), 1) == lo_col
    acc_parts = [dot_nn(hi_hot, piece) for piece in split3(acc_v[...])]
    acc_lines = acc_parts[0] + acc_parts[1] + acc_parts[2]
    old_acc = jnp.sum(jnp.where(lo_hit, acc_lines, 0.0), axis=1, keepdims=True)
    hi_hot_t = (
        (iota((acc_rows, slots_n), 0) == lax.div(touched_row, lanes)).astype(F32).astype(BF16)
    )
    hi_hot_ref[...] = hi_hot_t
    acc_hit = dot_nn(hi_hot_t, lo_hit.astype(F32).astype(BF16)) > 0.5
    acc_rest_ref[...] = jnp.where(acc_hit, 0.0, acc_v[...])

    place = (iota((rows_n, slots_n), 0) == touched_row).astype(F32).astype(BF16)
    place_ref[...] = place
    hits = dot_nn(place, jnp.ones((slots_n, table_v.shape[1]), BF16))
    rest_ref[...] = jnp.where(hits > 0.5, 0.0, table_v[...].astype(F32)).astype(BF16)

    n_p = len(plane_peers)
    pltpu.make_async_copy(
        plane_recv.at[pl.ds(0, n_p)], plane_recv.at[pl.ds(0, n_p)], plane_sem.at[1]
    ).wait()
    total = tree_sum([plane_recv[i] for i in range(n_p + 1)])

    d_sum = to_column(total[0:1, :] * click_row - total[1:2, :])
    acc_new = old_acc + d_sum * d_sum * unit_square
    rows_ref[...] = (old_rows - (learn_rate * d_sum * lax.rsqrt(acc_new)) * unit_grad).astype(BF16)
    acc_ref[...] = jnp.where(lo_hit, acc_new, 0.0)

    core_copy.wait_send()
    pltpu.make_async_copy(far_recv, far_recv, far_sent).wait()
    pltpu.make_async_copy(near_recv, near_recv, near_sem.at[0]).wait()
    pltpu.make_async_copy(
        plane_recv.at[pl.ds(0, n_p)], plane_recv.at[pl.ds(0, n_p)], plane_sem.at[0]
    ).wait()


def scatter_kernel(
    rows_ref, acc_ref, place_ref, rest_ref, hi_hot_ref, acc_rest_ref, table_out, acc_out, tiles, acc_tile, sem
):
    rows = rows_ref[...]
    count = tiles.shape[0]
    step = tiles.shape[1]
    copies = []
    for i in range(count):
        span = slice(i * step, (i + 1) * step)
        tiles[i] = (dot_nn(place_ref[span, :], rows) + rest_ref[span, :].astype(F32)).astype(BF16)
        copies.append(
            pltpu.make_async_copy(tiles.at[i], table_out.at[pl.ds(i * step, step)], sem.at[i + 1])
        )
        copies[-1].start()
        if i == count - 1:
            placed = [dot_nn(hi_hot_ref[...], piece) for piece in split3(acc_ref[...])]
            acc_tile[...] = acc_rest_ref[...] + (placed[0] + placed[1] + placed[2])
            copies.append(pltpu.make_async_copy(acc_tile, acc_out, sem.at[0]))
            copies[-1].start()
    for copy in copies:
        copy.wait()


def on_device(
    n_y,
    n_z,
    owner_shard,
    slot_index,
    lengths,
    labels,
    embed_table,
    accumulator,
    touched,
    w_in,
    w_mid,
    norm_gain,
    w_out,
):
    rows_n, emb = embed_table.shape
    slots_n = touched.shape[0]
    width = w_out.shape[0]
    lanes = 128
    acc2 = accumulator.reshape(rows_n // lanes, lanes)
    touched2 = touched.reshape(1, slots_n)
    hbm_spec = pl.BlockSpec(memory_space=pltpu.HBM)
    vmem = pl.BlockSpec(memory_space=pltpu.VMEM)
    n_far = UP + DOWN
    n_near = UP + REACH
    part = N_XHI * 2
    operands = [
        pltpu.with_memory_space_constraint(array, pltpu.HBM)
        for array in (
            owner_shard,
            slot_index,
            lengths,
            labels,
            embed_table,
            acc2,
            touched2,
            w_in,
            w_mid,
            norm_gain.reshape(1, width),
            w_out.reshape(1, width),
        )
    ]
    made = pl.pallas_call(
        functools.partial(reduce_kernel, n_y, n_z),
        out_shape=(
            jax.ShapeDtypeStruct((slots_n, emb), BF16),
            jax.ShapeDtypeStruct((slots_n, lanes), F32),
            jax.ShapeDtypeStruct((rows_n, slots_n), BF16),
            jax.ShapeDtypeStruct((rows_n, emb), BF16),
            jax.ShapeDtypeStruct((acc2.shape[0], slots_n), BF16),
            jax.ShapeDtypeStruct(acc2.shape, F32),
        ),
        in_specs=[hbm_spec] * len(operands),
        out_specs=(vmem,) * 6,
        scratch_shapes=[
            pltpu.VMEM(owner_shard.shape, jnp.int32),
            pltpu.VMEM(slot_index.shape, jnp.int32),
            pltpu.SMEM(lengths.shape, jnp.int32),
            pltpu.VMEM(labels.shape, F32),
            pltpu.VMEM(embed_table.shape, BF16),
            pltpu.VMEM(acc2.shape, F32),
            pltpu.VMEM(touched2.shape, jnp.int32),
            pltpu.VMEM(w_in.shape, BF16),
            pltpu.VMEM(w_mid.shape, BF16),
            pltpu.VMEM((1, width), F32),
            pltpu.VMEM((1, width), F32),
            pltpu.SemaphoreType.DMA((11,)),
            pltpu.VMEM((N_CORE * n_z, part, slots_n), F32),
            pltpu.VMEM((n_far, N_CORE, part, slots_n), F32),
            pltpu.VMEM((n_near, part, slots_n), F32),
            pltpu.VMEM((n_near, part, slots_n), F32),
            pltpu.VMEM((n_z, part, slots_n), F32),
            pltpu.VMEM((N_XHI, 2, slots_n), F32),
            pltpu.VMEM((N_XHI * n_y * N_XLO, 2, slots_n), F32),
            pltpu.SemaphoreType.DMA((n_far,)),
            pltpu.SemaphoreType.DMA,
            pltpu.SemaphoreType.DMA((2,)),
            pltpu.SemaphoreType.DMA((2,)),
            pltpu.SemaphoreType.DMA((2,)),
        ],
        compiler_params=pltpu.CompilerParams(
            collective_id=0, has_side_effects=True, vmem_limit_bytes=32 * 1024 * 1024
        ),
        name="reduce",
    )(*operands)
    tiles = 4
    table_out, accum_out = pl.pallas_call(
        scatter_kernel,
        out_shape=(
            jax.ShapeDtypeStruct(embed_table.shape, BF16),
            jax.ShapeDtypeStruct(acc2.shape, F32),
        ),
        in_specs=[vmem] * 6,
        out_specs=(hbm_spec,) * 2,
        scratch_shapes=[
            pltpu.VMEM((tiles, rows_n // tiles, emb), BF16),
            pltpu.VMEM(acc2.shape, F32),
            pltpu.SemaphoreType.DMA((tiles + 1,)),
        ],
        compiler_params=pltpu.CompilerParams(vmem_limit_bytes=24 * 1024 * 1024),
        name="scatter",
    )(*made)
    return (table_out, accum_out.reshape(rows_n))


def solution(mesh):
    n_y = mesh.shape["replica"] // N_XLO
    n_z = mesh.shape["mp"] // (N_CORE * N_XHI)
    in_specs = (
        P(("replica", "mp"), None),
        P(("replica", "mp"), None),
        P(("replica", "mp")),
        P(("replica", "mp"), None),
        P("mp", None),
        P("mp"),
        P("mp"),
        P(),
        P(),
        P(),
        P(),
    )
    out_specs = (P("mp", None), P("mp"))
    return jax.shard_map(
        functools.partial(on_device, n_y, n_z),
        mesh=mesh,
        in_specs=in_specs,
        out_specs=out_specs,
        check_vma=False,
    )
```
